128 devices in a mesh: seg: 8 (over y, core), sub: 16 (over x, z).
Axes of the slice: x: 4, y: 4, z: 4, core: 2. Of those that a mesh axis runs over, the one named last changes fastest.
Arguments:
- nodal_loads: float32 [8, 16, 32, 3072], P('seg', 'sub'), may hold values from -6 to 6
- schur_matrix: bfloat16 [8, 16, 3072, 3072], P('seg', 'sub'), may hold values from -2 to 9, as said below
- face_rows: int32 [8, 16, 3072], P('seg', 'sub'), may hold values from 0 to 3071, each once within a row
- face_len: int32 [8, 16, 2], replicated, may hold values from 192 to 768, as said below
- relax_step: float32 [8, 16], P('seg', 'sub'), may hold values from 0.03 to 0.1
- coarse_basis: float32 [8, 16, 4, 3072], P('seg', 'sub'), may hold values from -0.625 to 0.625
- primal_index: int32 [8, 16, 4], replicated, may hold values from 0 to 271, as said below
- coarse_inverse: float32 [272, 272], replicated, may hold values from -1 to 1.5, as said below
Outputs:
- solution: float32 [8, 16, 32, 3072], P('seg', 'sub')
- residual: float32 [8, 16, 32, 3072], P('seg', 'sub')
The draws below stay inside these ranges and needn't reach their ends.
Inputs may be any that keep to these rules, and one draw needn't show every extreme that they name: `schur_matrix`: symmetric in its last two dimensions and positive definite for each subdomain. `face_len`: entry [s, j, 0] counts the shared slots of the face between subdomains j and (j+1) mod 16 of segment s; entry [s, j, 1] those of the face between segments s and s+1 at subdomain j (not read for the last segment). Some entry [s, j, 0] equals 768. `primal_index`: one global number for each face: the face between subdomains j and (j+1) mod 16 of segment s, and the face below segment s at subdomain j (and above the last segment), numbered in a random order. Subdomains sharing a face name the same number; a face at the bridge's ends belongs to one subdomain only. `coarse_inverse`: symmetric positive definite.
All inputs are finite; a program needn't handle non-finite values.
Results may differ from the reference program's by a relative error of at most 0.0015.
Values sent between devices are 32-bit elements; how exact they have to be, the bound alone decides.
No kernel may reach another device: no remote copies, remote signals or barrier semaphores. Data moves between devices by JAX's collectives and lax.ppermute only.
A program may use at most 128 MiB of HBM per device.

```python
import math
import jax
import jax.numpy as jnp
from jax import lax

NI = 3072
K = 32
DEG = 3
ITERS = 3
NF = 768
NP = 272
N_SEG = 8
N_SUB = 16


def draw_schur_matrix(key, part):

    def single(number):
        sub_key = jax.random.fold_in(jax.random.fold_in(key, 17), number)
        key_diag, key_noise = jax.random.split(sub_key)
        scales = jnp.exp(jax.random.uniform(key_diag, (NI,), jnp.float32, math.log(1.6), math.log(8.0)))
        noise = jax.random.normal(key_noise, (NI, NI), jnp.float32)
        sym_noise = (noise + noise.T) / math.sqrt(2.0 * NI)
        core = jnp.eye(NI, dtype=jnp.float32) + 0.3 * sym_noise
        roots = jnp.sqrt(scales)
        return (roots[:, None] * core * roots[None, :]).astype(jnp.bfloat16)
    stacked = lax.map(single, jnp.arange(N_SEG * N_SUB, dtype=jnp.int32))
    return stacked.reshape(N_SEG, N_SUB, NI, NI)


def draw_face_len(key, part):
    key_len, key_seg, key_sub = jax.random.split(jax.random.fold_in(key, 23), 3)
    values = jax.random.randint(key_len, (N_SEG, N_SUB, 2), NF // 4, NF + 1, jnp.int32)
    seg_pick = jax.random.randint(key_seg, (), 0, N_SEG, jnp.int32)
    sub_pick = jax.random.randint(key_sub, (), 0, N_SUB, jnp.int32)
    return values.at[seg_pick, sub_pick, 0].set(NF)


def draw_primal_index(key, part):
    order = jax.random.permutation(jax.random.fold_in(key, 29), NP).astype(jnp.int32)
    seg_ids = jnp.arange(N_SEG, dtype=jnp.int32)[:, None]
    sub_ids = jnp.arange(N_SUB, dtype=jnp.int32)[None, :]
    left_face = seg_ids * N_SUB + (sub_ids + N_SUB - 1) % N_SUB
    right_face = seg_ids * N_SUB + sub_ids
    down_face = N_SEG * N_SUB + seg_ids * N_SUB + sub_ids
    up_face = N_SEG * N_SUB + (seg_ids + 1) * N_SUB + sub_ids
    faces = jnp.stack([left_face, right_face, down_face, up_face], axis=2)
    return order[faces].astype(jnp.int32)


def draw_coarse_inverse(key, part):
    key_diag, key_noise = jax.random.split(jax.random.fold_in(key, 31))
    scales = jnp.exp(jax.random.uniform(key_diag, (NP,), jnp.float32, math.log(0.2), 0.0))
    noise = jax.random.normal(key_noise, (NP, NP), jnp.float32)
    sym_noise = (noise + noise.T) / math.sqrt(2.0 * NP)
    core = jnp.eye(NP, dtype=jnp.float32) + 0.3 * sym_noise
    roots = jnp.sqrt(scales)
    return roots[:, None] * core * roots[None, :]


def level_of(own_key, extent, cuts, smallest, largest):
    factor_of = 1.0
    for position, blocks in cuts:
        draws = jax.random.uniform(jax.random.fold_in(jax.random.fold_in(own_key, 6), position), (blocks,), jnp.float32, smallest / len(cuts), largest / len(cuts))
        factor_of = factor_of * jnp.repeat(jnp.exp(draws), extent[position] // blocks).reshape((-1,) + (1,) * (len(extent) - 1 - position))
    return factor_of


def centred(rng, extent, deviation, most, cuts=(), held_as=jnp.bfloat16):
    result = deviation * jax.random.normal(rng, extent, jnp.float32)
    if cuts:
        result = result * level_of(rng, extent, cuts, -0.22, 0.18)
    return jnp.clip(result, -most, most).astype(held_as)


def setup_inputs(seed: int = 0) -> dict:
    keys = jax.random.split(jax.random.key(seed), 9)
    return {
        "nodal_loads": centred(keys[0], (N_SEG, N_SUB, K, NI), 1.0, 6.0, ((0, 8), (1, 16)), jnp.float32),
        "schur_matrix": draw_schur_matrix(jax.random.fold_in(keys[8], 71), 0),
        "face_rows": jax.vmap(lambda own: jax.random.permutation(own, NI))(jax.random.split(keys[2], N_SEG * N_SUB)).reshape((N_SEG, N_SUB, NI)).astype(jnp.int32),
        "face_len": draw_face_len(jax.random.fold_in(keys[8], 71), 0),
        "relax_step": jnp.clip(jnp.exp(math.log(0.1) - 1.2039728 * jax.random.uniform(keys[4], (N_SEG, N_SUB), jnp.float32) ** level_of(keys[4], (N_SEG, N_SUB), ((0, 8), (1, 16)), -0.2, 0.2)), 0.03, 0.1),
        "coarse_basis": centred(keys[5], (N_SEG, N_SUB, 4, NI), (NI // 36) ** -0.5, 0.625, ((0, 8), (1, 16)), jnp.float32),
        "primal_index": draw_primal_index(jax.random.fold_in(keys[8], 71), 0),
        "coarse_inverse": draw_coarse_inverse(jax.random.fold_in(keys[8], 71), 0),
    }


HIGH = lax.Precision.HIGHEST

def symmetric(matrix):
    return 0.5 * (matrix + matrix.T)

def split_product(values, matrix):
    upper = values.astype(jnp.bfloat16)
    upper_back = lax.optimization_barrier(upper).astype(jnp.float32)
    lower = (values - upper_back).astype(jnp.bfloat16)
    first = jnp.dot(upper.astype(jnp.float32), matrix.astype(jnp.float32), preferred_element_type=jnp.float32)
    second = jnp.dot(lower.astype(jnp.float32), matrix.astype(jnp.float32), preferred_element_type=jnp.float32)
    return first + second

def reference(nodal_loads, schur_matrix, face_rows, face_len, relax_step, coarse_basis, primal_index, coarse_inverse):
    count = N_SEG * N_SUB
    flat_rows = face_rows.reshape(count, NI).astype(jnp.int32)
    face_len = face_len.astype(jnp.int32)
    zero_row = jnp.zeros((1, N_SUB), jnp.int32)
    lengths = jnp.stack([jnp.roll(face_len[:, :, 0], 1, axis=1), face_len[:, :, 0], jnp.concatenate([zero_row, face_len[:-1, :, 1]], axis=0), jnp.concatenate([face_len[:-1, :, 1], zero_row], axis=0)], axis=2).astype(jnp.int32)
    live_mask = (jnp.arange(NF, dtype=jnp.int32)[None, None, None, :] < lengths[..., None]).astype(jnp.float32)
    batch_ids = jnp.arange(count, dtype=jnp.int32)[:, None]
    weight_flat = jnp.zeros((count, NI), jnp.float32).at[batch_ids, flat_rows].set(jnp.float32(1.0) - jnp.float32(0.5) * live_mask.reshape(count, NI))
    inverse_rows = jnp.zeros((count, NI), jnp.int32).at[batch_ids, flat_rows].set(jnp.broadcast_to(jnp.arange(NI, dtype=jnp.int32)[None, :], (count, NI)))
    live_weight = weight_flat.reshape(N_SEG, N_SUB, 1, NI)
    schur_flat = schur_matrix.reshape(count, NI, NI)
    step_full = relax_step[:, :, None, None]
    face_ids = primal_index.reshape(count, 4).astype(jnp.int32)

    def assemble(values):
        flat = values.reshape(count, K, NI)
        slots = jnp.take_along_axis(flat, flat_rows[:, None, :], axis=2)
        slots = slots.reshape(N_SEG, N_SUB, K, 4, NF) * live_mask[:, :, None]
        zeros_plane = jnp.zeros_like(slots[:1, :, :, 0])
        left_in = jnp.roll(slots[:, :, :, 1], 1, axis=1)
        right_in = jnp.roll(slots[:, :, :, 0], -1, axis=1)
        down_in = jnp.concatenate([zeros_plane, slots[:-1, :, :, 3]], axis=0)
        up_in = jnp.concatenate([slots[1:, :, :, 2], zeros_plane], axis=0)
        received = jnp.stack([left_in, right_in, down_in, up_in], axis=3) * live_mask[:, :, None]
        received = received.reshape(count, K, NI)
        back = jnp.take_along_axis(received, inverse_rows[:, None, :], axis=2)
        return (flat + back).reshape(values.shape)

    def local_product(values):
        flat = values.reshape(count, K, NI)
        out = lax.map(lambda pair: split_product(pair[0], pair[1]), (flat, schur_flat))
        return out.reshape(values.shape)

    def inner(left, right):
        return jnp.einsum('abkn,abln->kl', left * live_weight, right, precision=HIGH)

    def precondition(resid):
        weighted = resid * live_weight
        solve = step_full * weighted
        for sweep in range(DEG):
            solve = step_full * weighted + solve - step_full * local_product(solve)
        local_coarse = jnp.einsum('abkn,abcn->abkc', weighted, coarse_basis, precision=HIGH)
        spread = jnp.transpose(local_coarse.reshape(count, K, 4), (1, 0, 2)).reshape(K, count * 4)
        coarse_sum = jnp.zeros((K, NP), jnp.float32).at[:, face_ids.reshape(-1)].add(spread)
        coarse_solution = jnp.dot(coarse_sum, coarse_inverse, precision=HIGH)
        picked = jnp.take(coarse_solution, face_ids, axis=1)
        picked = jnp.transpose(picked, (1, 0, 2)).reshape(N_SEG, N_SUB, K, 4)
        correction = jnp.einsum('abkc,abcn->abkn', picked, coarse_basis, precision=HIGH)
        return assemble((solve + correction) * live_weight)
    solution = jnp.zeros_like(nodal_loads)
    residual = assemble(nodal_loads)
    precond = precondition(residual)
    direction = precond
    rho = symmetric(inner(precond, residual))
    for iteration in range(ITERS):
        image = assemble(local_product(direction))
        curvature = symmetric(inner(direction, image))
        factor = jnp.linalg.cholesky(curvature)
        alpha = jax.scipy.linalg.cho_solve((factor, True), rho)
        solution = solution + jnp.einsum('kl,abkn->abln', alpha, direction, precision=HIGH)
        residual = residual - jnp.einsum('kl,abkn->abln', alpha, image, precision=HIGH)
        if iteration + 1 < ITERS:
            precond = precondition(residual)
            rho_next = symmetric(inner(precond, residual))
            factor_rho = jnp.linalg.cholesky(rho)
            beta = jax.scipy.linalg.cho_solve((factor_rho, True), rho_next)
            direction = precond + jnp.einsum('kl,abkn->abln', beta, direction, precision=HIGH)
            rho = rho_next
    return (solution, residual)
```

```python
import functools

import jax
import jax.numpy as jnp
from jax import lax
from jax.experimental import pallas as pl
from jax.experimental.pallas import tpu as pltpu
from jax.sharding import PartitionSpec as P

DEG = 3
ITERS = 3
HIGH = lax.Precision.HIGHEST
F32 = jnp.float32
BF16 = jnp.bfloat16
MIB = 1 << 20

PLACE = 128


def dot(a, b):
    return jnp.dot(a, b, precision=HIGH, preferred_element_type=F32)


def dot_nt(a, b, precision=HIGH):
    return lax.dot_general(a, b, (((1,), (1,)), ((), ())), precision=precision, preferred_element_type=F32)


def symmetric(matrix):
    return 0.5 * (matrix + matrix.T)


def two_terms(x):
    hi = x.astype(BF16)
    return hi, (x - hi.astype(F32)).astype(BF16)


def three_terms(x):
    hi = x.astype(BF16)
    rest = x - hi.astype(F32)
    mid = rest.astype(BF16)
    return hi, mid, (rest - mid.astype(F32)).astype(BF16)


def put_terms(ref, first, columns, terms):
    rows = terms[0].shape[0]
    for at, term in enumerate(terms):
        ref[first + at * rows : first + (at + 1) * rows, columns] = term


def cut(width, parts):
    return width // parts if width % parts == 0 and (width // parts) % 128 == 0 else width // 4


def spd_solve(a, b):
    n = a.shape[0]
    both = jnp.concatenate([a, b], axis=1)
    row = lax.broadcasted_iota(jnp.int32, (n, 1), 0)
    for k in range(n):
        pivot = both[k : k + 1, :] / both[k : k + 1, k : k + 1]
        both = jnp.where(row == k, pivot, both - both[:, k : k + 1] * pivot)
    return both[:, n:]


def permute(terms_ref, index_ref, rows, emit):
    width = index_ref.shape[1]
    tile = cut(width, 8)

    def one(t, carry):
        columns = pl.ds(pl.multiple_of(t * tile, tile), tile)
        hot = (lax.broadcasted_iota(jnp.int32, (width, tile), 0) == index_ref[0:1, columns]).astype(F32).astype(BF16)
        y = jnp.dot(terms_ref[0 : 3 * rows, :], hot, preferred_element_type=F32)
        emit(columns, (y[:rows] + y[rows : 2 * rows]) + y[2 * rows : 3 * rows])
        return carry

    lax.fori_loop(0, width // tile, one, 0)


def face_mask(len_ref, face, face_width):
    at = lax.broadcasted_iota(jnp.int32, (1, face_width), 1)
    return (at < len_ref[face]).astype(F32)


def gather_slots(x, terms_ref, rows_ref, len_ref, hold_ref, out_refs):
    rows = x.shape[0]
    put_terms(terms_ref, 0, slice(None), three_terms(x))

    def emit(columns, y):
        hold_ref[0:rows, columns] = y

    permute(terms_ref, rows_ref, rows, emit)
    face_width = rows_ref.shape[1] // 4
    for face, out in enumerate(out_refs):
        keep = out.shape[0]
        part = hold_ref[0:keep, face * face_width : (face + 1) * face_width]
        out[...] = part * face_mask(len_ref, face, face_width)


def scatter_faces(in_refs, terms_ref, inverse_ref, emit):
    face_width = inverse_ref.shape[1] // 4
    for face, ref in enumerate(in_refs):
        put_terms(terms_ref, 0, slice(face * face_width, (face + 1) * face_width), three_terms(ref[...]))
    permute(terms_ref, inverse_ref, in_refs[0].shape[0], emit)


def product(terms, matrix_ref, emit):
    width = matrix_ref.shape[1]
    tile = cut(width, 3)
    half = terms.shape[0] // 2

    def one(t, carry):
        columns = pl.ds(pl.multiple_of(t * tile, tile), tile)
        y = jnp.dot(terms[...], matrix_ref[:, columns], preferred_element_type=F32)
        emit(columns, y[:half] + y[half:])
        return carry

    lax.fori_loop(0, width // tile, one, 0)


def local_solve(weighted_ref, solve_ref, terms_ref, relax, matrix_ref):
    solve_ref[...] = relax * weighted_ref[...]
    for sweep in range(DEG):
        put_terms(terms_ref, 0, slice(None), two_terms(solve_ref[...]))

        def emit(columns, y):
            solve_ref[:, columns] = relax * weighted_ref[:, columns] + solve_ref[:, columns] - relax * y

        product(terms_ref.at[0 : 2 * solve_ref.shape[0]], matrix_ref, emit)


def place(columns, index_ref, members, width):
    at = lax.broadcasted_iota(jnp.int32, (1, width), 1)
    total = jnp.zeros((columns.shape[0], width), F32)
    for member in members:
        total = total + columns[:, member : member + 1] * (at == index_ref[member]).astype(F32)
    return total


def correct(solve, coarse_solution, index_ref, basis_ref):
    at = lax.broadcasted_iota(jnp.int32, (1, coarse_solution.shape[1]), 1)
    for face in range(4):
        mine = (at == index_ref[face]).astype(F32)
        picked = jnp.sum(coarse_solution * mine, axis=1, keepdims=True)
        solve = solve + picked * basis_ref[face : face + 1, :]
    return solve


def first_gather(len_ref, loads_ref, basis_ref, rows_ref, o0, o1, o2, o3, terms_ref, hold_ref):
    block = loads_ref.shape[0]
    spare = jnp.zeros((8, loads_ref.shape[1]), F32)
    x = jnp.concatenate([loads_ref[...], 0.5 * basis_ref[...], spare], axis=0)
    gather_slots(x, terms_ref, rows_ref, len_ref, hold_ref, (o0, o1, o2, o3))


def first_scatter(
    len_ref, index_ref, loads_ref, basis_ref, rows_ref, i0, i1, i2, i3,
    residual_ref, reach_ref, weight_ref, inverse_ref, coarse_ref, terms_ref,
):
    block, width = loads_ref.shape
    face_width = width // 4
    tile = cut(width, 12)
    for face, ref in enumerate((i0, i1, i2, i3)):
        columns = slice(face * face_width, (face + 1) * face_width)
        put_terms(terms_ref, 0, columns, three_terms(ref[0:block, :]))
        got = ref[block : block + 8, :]
        blank = jnp.zeros((4, face_width), F32)
        spread = jnp.concatenate([got[0:4] if at == face else blank for at in range(4)], axis=0)
        put_terms(terms_ref, 3 * block, columns, three_terms(spread))
        row = lax.broadcasted_iota(jnp.int32, (16, face_width), 0)
        slot = lax.broadcasted_iota(jnp.int32, (16, face_width), 1) + face * face_width
        weight = 1.0 - 0.5 * face_mask(len_ref, face, face_width)
        extra = jnp.where(
            row == 0,
            weight,
            jnp.where(row == 1, (slot // 256).astype(F32), jnp.where(row == 2, (slot % 256).astype(F32), 0.0)),
        )
        terms_ref[3 * block + 48 : 3 * block + 64, columns] = extra.astype(BF16)

    def one(t, carry):
        columns = pl.ds(pl.multiple_of(t * tile, tile), tile)
        own = lax.broadcasted_iota(jnp.int32, (tile, width), 0) + t * tile
        hot = (own == rows_ref[0:1, :]).astype(F32).astype(BF16)
        y = dot_nt(terms_ref[...], hot, None)
        residual_ref[:, columns] = loads_ref[:, columns] + ((y[:block] + y[block : 2 * block]) + y[2 * block : 3 * block])
        near = y[3 * block : 3 * block + 48]
        extra = y[3 * block + 48 : 3 * block + 64]
        weight = extra[0:1]
        weight_ref[:, columns] = weight
        inverse_ref[:, columns] = (extra[1:2] * 256.0 + extra[2:3]).astype(jnp.int32)
        reach_ref[0:8, columns] = weight * basis_ref[:, columns]
        reach_ref[8:24, columns] = (near[:16] + near[16:32]) + near[32:48]
        return carry

    lax.fori_loop(0, width // tile, one, 0)
    coarse = dot_nt(residual_ref[...] * weight_ref[...], basis_ref[...])
    coarse_ref[...] = place(coarse, index_ref, range(4), coarse_ref.shape[1])


def first_solve(relax_ref, residual_ref, weight_ref, matrix_ref, solve_ref, rho_ref, terms_ref, weighted_ref):
    weighted_ref[...] = residual_ref[...] * weight_ref[...]
    local_solve(weighted_ref, solve_ref, terms_ref, relax_ref[0, 0], matrix_ref)
    rho_ref[...] = dot_nt(solve_ref[...], weighted_ref[...])


def first_correct(
    len_ref, index_ref, solve_ref, coarse_ref, coarse_inverse_ref, basis_ref, weight_ref, rows_ref,
    own_ref, coarse_rho_ref, o0, o1, o2, o3, terms_ref, hold_ref,
):
    coarse = coarse_ref[...]
    coarse_solution = dot(coarse, coarse_inverse_ref[...])
    coarse_rho_ref[...] = dot_nt(coarse_solution, coarse)
    own = correct(solve_ref[...], coarse_solution, index_ref, basis_ref) * weight_ref[...]
    own_ref[...] = own
    gather_slots(own, terms_ref, rows_ref, len_ref, hold_ref, (o0, o1, o2, o3))


def apply_matrix(first, *refs):
    refs = list(refs)
    len_ref, index_ref, own_ref, rho_ref, matrix_ref, reach_ref, rows_ref, inverse_ref = refs[:8]
    ins, rest = refs[8:12], refs[12:]
    direction_ref = None if first else rest.pop(0)
    precond_ref, partial_ref, sums_ref, o0, o1, o2, o3, terms_ref, hold_ref = rest
    block = own_ref.shape[0]

    def gain(columns, y):
        precond_ref[:, columns] = own_ref[:, columns] + y

    scatter_faces(ins, terms_ref, inverse_ref, gain)
    precond = precond_ref[...]
    put_terms(terms_ref, 0, slice(None), two_terms(precond))

    def emit(columns, y):
        partial_ref[:, columns] = y

    product(terms_ref.at[0 : 2 * block], matrix_ref, emit)
    partial = partial_ref[...]
    sums_ref[:, 0:PLACE] = jnp.zeros((block, PLACE), F32)
    sums_ref[:, 0:block] = rho_ref[...]
    sums_ref[:, block : 2 * block] = dot_nt(partial, precond)
    if not first:
        sums_ref[:, 2 * block : 3 * block] = dot_nt(partial, direction_ref[...])
    coarse = dot_nt(partial, reach_ref[...])
    members = (0, 1, 2, 3) + tuple(range(8, 24))
    sums_ref[:, PLACE:] = place(coarse, index_ref, members, sums_ref.shape[1] - PLACE)
    gather_slots(partial, terms_ref, rows_ref, len_ref, hold_ref, (o0, o1, o2, o3))


def advance(first, last, *refs):
    refs = list(refs)
    sums_ref, coarse_rho_ref, precond_ref, partial_ref, residual_ref, inverse_ref = refs[:6]
    ins, rest = refs[6:10], refs[10:]
    if not first:
        solution_ref, old_direction_ref, old_image_ref, old_curvature_ref, old_rho_ref = rest[:5]
        rest = rest[5:]
    if not last:
        if not first:
            old_coarse_image_ref = rest.pop(0)
        len_ref, index_ref, relax_ref, matrix_ref, weight_ref, basis_ref, rows_ref, coarse_ref, coarse_inverse_ref = rest[:9]
        rest = rest[9:]
        new_solution_ref, new_residual_ref, direction_ref, image_ref, curvature_out_ref, rho_out_ref = rest[:6]
        coarse_image_ref, new_coarse_ref, own_ref, new_coarse_rho_ref, local_rho_ref, o0, o1, o2, o3 = rest[6:15]
        terms_ref, hold_ref, weighted_ref = rest[15:]
    else:
        new_solution_ref, new_residual_ref, terms_ref, image_ref = rest
    block = precond_ref.shape[0]

    def gain(columns, y):
        image_ref[:, columns] = partial_ref[:, columns] + y

    scatter_faces(ins, terms_ref, inverse_ref, gain)
    rho = symmetric(sums_ref[:, 0:block] + coarse_rho_ref[...])
    curvature = symmetric(sums_ref[:, block : 2 * block])
    direction = precond_ref[...]
    image = image_ref[...]
    if not first:
        beta = spd_solve(old_rho_ref[...], rho)
        back = beta.T
        cross = dot(sums_ref[:, 2 * block : 3 * block], beta)
        curvature = curvature + (cross + cross.T) + symmetric(dot(back, dot(old_curvature_ref[...], beta)))
        direction = direction + dot(back, old_direction_ref[...])
        image = image + dot(back, old_image_ref[...])
    step = spd_solve(curvature, rho).T
    moved = dot(step, direction)
    new_solution_ref[...] = moved if first else solution_ref[...] + moved
    residual = residual_ref[...] - dot(step, image)
    new_residual_ref[...] = residual
    if last:
        return
    direction_ref[...] = direction
    image_ref[...] = image
    curvature_out_ref[...] = curvature
    rho_out_ref[...] = rho
    coarse_image = sums_ref[:, PLACE:]
    if not first:
        coarse_image = coarse_image + dot(back, old_coarse_image_ref[...])
    coarse_image_ref[...] = coarse_image
    coarse = coarse_ref[...] - dot(step, coarse_image)
    new_coarse_ref[...] = coarse
    coarse_solution = dot(coarse, coarse_inverse_ref[...])
    new_coarse_rho_ref[...] = dot_nt(coarse_solution, coarse)
    weighted_ref[...] = residual * weight_ref[...]
    local_solve(weighted_ref, own_ref, terms_ref, relax_ref[0, 0], matrix_ref)
    local_rho_ref[...] = dot_nt(own_ref[...], weighted_ref[...])
    own = correct(own_ref[...], coarse_solution, index_ref, basis_ref) * weight_ref[...]
    own_ref[...] = own
    gather_slots(own, terms_ref, rows_ref, len_ref, hold_ref, (o0, o1, o2, o3))


def on_core(kernel, args, scalars, outs, scratch, flops, limit=20 * MIB):
    specs = [pl.BlockSpec(memory_space=pltpu.SMEM if at in scalars else pltpu.VMEM) for at in range(len(args))]
    size = sum(x.size * x.dtype.itemsize for x in args) + sum(4 * o.size for o in outs)
    return pl.pallas_call(
        kernel,
        out_shape=outs,
        in_specs=specs,
        out_specs=[pl.BlockSpec(memory_space=pltpu.VMEM)] * len(outs),
        scratch_shapes=scratch,
        compiler_params=pltpu.CompilerParams(vmem_limit_bytes=limit),
        cost_estimate=pl.CostEstimate(flops=flops, bytes_accessed=size, transcendentals=0),
    )(*args)


def hop(x, axis, target):
    count = lax.axis_size(axis)
    return lax.ppermute(x, axis, [(i, target(i)) for i in range(count)])


def exchange(faces):
    subs, segs = lax.axis_size("sub"), lax.axis_size("seg")
    return [
        hop(faces[1], "sub", lambda i: (i + 1) % subs),
        hop(faces[0], "sub", lambda i: (i - 1) % subs),
        lax.ppermute(faces[3], "seg", [(i, i + 1) for i in range(segs - 1)]),
        lax.ppermute(faces[2], "seg", [(i + 1, i) for i in range(segs - 1)]),
    ]


def total(x):
    x = x + hop(x, "seg", lambda i: i ^ 1)
    x = x + sum(hop(x, "seg", lambda i, k=k: (i // 2 + k) % 4 * 2 + i % 2) for k in (1, 2, 3))
    x = x + sum(hop(x, "sub", lambda i, k=k: i // 4 * 4 + (i % 4 + k) % 4) for k in (1, 2, 3))
    return x + sum(hop(x, "sub", lambda i, k=k: (i // 4 + k) % 4 * 4 + i % 4) for k in (1, 2, 3))


def body(nodal_loads, schur_matrix, face_rows, face_len, relax_step, coarse_basis, primal_index, coarse_inverse):
    s, j = lax.axis_index("seg"), lax.axis_index("sub")
    segs, subs = lax.axis_size("seg"), lax.axis_size("sub")
    loads, matrix, rows = nodal_loads[0, 0], schur_matrix[0, 0], face_rows[0]
    block, width = loads.shape
    face_width = width // 4
    basis = jnp.pad(coarse_basis[0, 0], ((0, 4), (0, 0)))
    padded = -(-coarse_inverse.shape[0] // 128) * 128
    extra = padded - coarse_inverse.shape[0]
    inverse_full = jnp.pad(coarse_inverse, ((0, extra), (0, extra)))
    left, right = (j + subs - 1) % subs, (j + 1) % subs
    down, up = jnp.maximum(s - 1, 0), jnp.minimum(s + 1, segs - 1)
    seg_of = jnp.stack([s, s, down, s])
    sub_of = jnp.stack([left, j, j, j])
    flat = (seg_of * subs + sub_of) * 2 + jnp.array([0, 0, 1, 1])
    there = jnp.stack([s >= 0, s >= 0, s > 0, s < segs - 1])
    lengths = jnp.where(there, jnp.take(face_len.reshape(-1), flat, mode="clip"), 0)
    cell = jnp.stack([s * subs + j, s * subs + j, s * subs + left, s * subs + right, down * subs + j, up * subs + j])
    index = jnp.take(primal_index.reshape(segs * subs, 4), cell, axis=0, mode="clip").reshape(-1)

    shape = lambda *size: jax.ShapeDtypeStruct(size, F32)
    full, small, coarse_block = shape(block, width), shape(block, block), shape(block, padded)
    terms = pltpu.VMEM((3 * block, width), BF16)
    hold = pltpu.VMEM((block, width), F32)
    faces = [shape(block, face_width)] * 4
    move = 2 * 3 * block * width * width
    turn = 2 * 2 * block * width * width

    wide = [shape(block + 8, face_width)] * 4
    slots = on_core(
        first_gather, (lengths, loads, basis, rows), (0,), wide,
        [pltpu.VMEM((3 * (block + 16), width), BF16), pltpu.VMEM((block + 16, width), F32)], move,
    )
    got = exchange(slots)
    residual, reach, weight, inverse, coarse = on_core(
        first_scatter, (lengths, index, loads, basis, rows, *got), (0, 1),
        [full, shape(24, width), shape(1, width), jax.ShapeDtypeStruct((1, width), jnp.int32), coarse_block],
        [pltpu.VMEM((3 * block + 64, width), BF16)], move,
    )
    coarse = total(coarse)
    solve, local_rho = on_core(
        first_solve, (relax_step, residual, weight, matrix), (0,), [full, small],
        [pltpu.VMEM((2 * block, width), BF16), hold], 3 * turn,
    )
    own, coarse_rho, *slots = on_core(
        first_correct, (lengths, index, solve, coarse, inverse_full, basis, weight, rows), (0, 1),
        [full, small, *faces], [terms, hold], move,
    )
    direction = image = answer = curvature = rho = coarse_image = None
    for iteration in range(ITERS):
        first, last = iteration == 0, iteration + 1 == ITERS
        got = exchange(slots)
        old = () if first else (direction,)
        precond, partial, sums, *slots = on_core(
            functools.partial(apply_matrix, first),
            (lengths, index, own, local_rho, matrix, reach, rows, inverse, *got, *old), (0, 1),
            [full, full, shape(block, PLACE + padded), *faces], [terms, hold], turn + 2 * move,
        )
        got = exchange(slots)
        sums = total(sums)
        args = [sums, coarse_rho, precond, partial, residual, inverse, *got]
        if not first:
            args += [answer, direction, image, curvature, rho]
        if last:
            answer, residual = on_core(
                functools.partial(advance, first, last), args, (), [full, full], [terms, hold], move,
            )
            break
        if not first:
            args += [coarse_image]
        at = len(args)
        args += [lengths, index, relax_step, matrix, weight, basis, rows, coarse, inverse_full]
        (answer, residual, direction, image, curvature, rho, coarse_image, coarse, own, coarse_rho, local_rho,
         *slots) = on_core(
            functools.partial(advance, first, last), args, (at, at + 1, at + 2),
            [full, full, full, full, small, small, coarse_block, coarse_block, full, small, small, *faces],
            [terms, hold, hold], 3 * turn + 2 * move,
        )
    return (answer[None, None], residual[None, None])


def solution(mesh):
    placed = (
        P("seg", "sub", None, None),
        P("seg", "sub", None, None),
        P("seg", "sub", None),
        P(),
        P("seg", "sub"),
        P("seg", "sub", None, None),
        P(),
        P(),
    )
    return jax.shard_map(
        body,
        mesh=mesh,
        in_specs=placed,
        out_specs=(P("seg", "sub", None, None), P("seg", "sub", None, None)),
        check_vma=False,
    )
```

```python
import functools

import jax
import jax.numpy as jnp
from jax import lax
from jax.experimental import pallas as pl
from jax.experimental.pallas import tpu as pltpu
from jax.sharding import PartitionSpec as P

DEG = 3
ITERS = 3
HIGH = lax.Precision.HIGHEST
F32 = jnp.float32
BF16 = jnp.bfloat16
MIB = 1 << 20

PLACE = 128
FACE = 4
INDEX = 8


def dot(a, b):
    return jnp.dot(a, b, precision=HIGH, preferred_element_type=F32)


def symmetric(matrix):
    return 0.5 * (matrix + matrix.T)


def two_terms(x):
    hi = x.astype(BF16)
    return hi, (x - hi.astype(F32)).astype(BF16)


def three_terms(x):
    hi = x.astype(BF16)
    rest = x - hi.astype(F32)
    mid = rest.astype(BF16)
    return hi, mid, (rest - mid.astype(F32)).astype(BF16)


def put_terms(ref, first, columns, terms):
    rows = terms[0].shape[0]
    for at, term in enumerate(terms):
        ref[first + at * rows : first + (at + 1) * rows, columns] = term


def fold(y, parts):
    rows = y.shape[0] // parts
    total = y[:rows]
    for at in range(1, parts):
        total = total + y[at * rows : (at + 1) * rows]
    return total


def gram(left, right, left_parts, right_parts):
    y = lax.dot_general(left, right, (((1,), (1,)), ((), ())), preferred_element_type=F32)
    y = fold(y, left_parts)
    columns = y.shape[1] // right_parts
    total = y[:, :columns]
    for at in range(1, right_parts):
        total = total + y[:, at * columns : (at + 1) * columns]
    return total


def stacked(matrix):
    return jnp.concatenate([jnp.concatenate([term] * 3, axis=1) for term in three_terms(matrix)], axis=0)


def mix(stack, x):
    terms = jnp.concatenate(three_terms(x), axis=0)
    return fold(jnp.dot(stack, terms, preferred_element_type=F32), 3)


def cut(width, parts):
    return width // parts if width % parts == 0 and (width // parts) % 128 == 0 else width // 4


def over_columns(width, parts, one):
    tile = cut(width, parts)

    def step(t, carry):
        start = pl.multiple_of(t * tile, tile)
        one(pl.ds(start, tile), start, tile)
        return carry

    lax.fori_loop(0, width // tile, step, 0)


def spd_solve(a, b):
    n = a.shape[0]
    both = jnp.concatenate([a, b], axis=1)
    row = lax.broadcasted_iota(jnp.int32, (n, 1), 0)
    for k in range(n):
        pivot = both[k : k + 1, :] / both[k : k + 1, k : k + 1]
        both = jnp.where(row == k, pivot, both - both[:, k : k + 1] * pivot)
    return both[:, n:]


def permute(terms_ref, index_ref, emit):
    width = index_ref.shape[1]

    def one(columns, start, tile):
        hot = (lax.broadcasted_iota(jnp.int32, (width, tile), 0) == index_ref[0:1, columns]).astype(F32).astype(BF16)
        emit(columns, fold(jnp.dot(terms_ref[...], hot, preferred_element_type=F32), 3))

    over_columns(width, 12, one)


def face_columns(table_ref, swap, face_width):
    return pl.ds(pl.multiple_of(table_ref[FACE + swap] * face_width, face_width), face_width)


def gather_slots(x, terms_ref, rows_ref, table_ref, hold_ref, out_refs):
    put_terms(terms_ref, 0, slice(None), three_terms(x))

    def emit(columns, y):
        hold_ref[:, columns] = y

    permute(terms_ref, rows_ref, emit)
    face_width = rows_ref.shape[1] // 4
    at = lax.broadcasted_iota(jnp.int32, (1, face_width), 1)
    for swap, out in enumerate(out_refs):
        part = hold_ref[0 : out.shape[0], face_columns(table_ref, swap, face_width)]
        out[...] = part * (at < table_ref[swap]).astype(F32)


def scatter_faces(in_refs, terms_ref, inverse_ref, table_ref, emit):
    face_width = inverse_ref.shape[1] // 4
    for swap, ref in enumerate(in_refs):
        put_terms(terms_ref, 0, face_columns(table_ref, swap, face_width), three_terms(ref[...]))
    permute(terms_ref, inverse_ref, emit)


def product(terms_ref, matrix_ref, emit):
    def one(columns, start, tile):
        emit(columns, fold(jnp.dot(terms_ref[...], matrix_ref[:, columns], preferred_element_type=F32), 2))

    over_columns(matrix_ref.shape[1], 3, one)


def sweep(weighted_ref, solve_ref, terms_ref, relax, matrix_ref):
    put_terms(terms_ref, 0, slice(None), two_terms(solve_ref[...]))

    def emit(columns, y):
        solve_ref[:, columns] = relax * weighted_ref[:, columns] + solve_ref[:, columns] - relax * y

    product(terms_ref, matrix_ref, emit)


def place(columns, table_ref, members, width):
    at = lax.broadcasted_iota(jnp.int32, (1, width), 1)
    total = jnp.zeros((columns.shape[0], width), F32)
    for member in members:
        total = total + columns[:, member : member + 1] * (at == table_ref[INDEX + member]).astype(F32)
    return total


def correct(solve_ref, coarse_solution, table_ref, basis_ref, weight_ref):
    at = lax.broadcasted_iota(jnp.int32, (1, coarse_solution.shape[1]), 1)
    solve = solve_ref[...]
    for face in range(4):
        mine = (at == table_ref[INDEX + face]).astype(F32)
        picked = jnp.sum(coarse_solution * mine, axis=1, keepdims=True)
        solve = solve + picked * basis_ref[face : face + 1, :]
    return solve * weight_ref[...]


def first_gather(table_ref, loads_ref, basis_ref, rows_ref, o0, o1, o2, o3, terms_ref, hold_ref):
    spare = jnp.zeros((12, loads_ref.shape[1]), F32)
    x = jnp.concatenate([loads_ref[...], 0.5 * basis_ref[...], spare], axis=0)
    gather_slots(x, terms_ref, rows_ref, table_ref, hold_ref, (o0, o1, o2, o3))


def first_scatter(
    table_ref, loads_ref, basis_ref, rows_ref, i0, i1, i2, i3,
    residual_ref, weighted_ref, reach_ref, weight_ref, inverse_ref, coarse_ref, terms_ref,
):
    block, width = loads_ref.shape
    face_width = width // 4
    row = lax.broadcasted_iota(jnp.int32, (16, face_width), 0)
    column = lax.broadcasted_iota(jnp.int32, (16, face_width), 1)
    for swap, ref in enumerate((i0, i1, i2, i3)):
        columns = face_columns(table_ref, swap, face_width)
        face = table_ref[FACE + swap]
        put_terms(terms_ref, 0, columns, three_terms(ref[0:block, :]))
        got = ref[block : block + 4, :]
        spread = jnp.where(row // 4 == face, jnp.concatenate([got] * 4, axis=0), 0.0)
        put_terms(terms_ref, 3 * block, columns, three_terms(spread))
        slot = column + face * face_width
        weight = 1.0 - 0.5 * (column < table_ref[swap]).astype(F32)
        extra = jnp.where(
            row == 0,
            weight,
            jnp.where(row == 1, (slot // 256).astype(F32), jnp.where(row == 2, (slot % 256).astype(F32), 0.0)),
        )
        terms_ref[3 * block + 48 : 3 * block + 64, columns] = extra.astype(BF16)

    def one(columns, start, tile):
        own = lax.broadcasted_iota(jnp.int32, (tile, width), 0) + start
        hot = (own == rows_ref[0:1, :]).astype(F32).astype(BF16)
        y = lax.dot_general(terms_ref[...], hot, (((1,), (1,)), ((), ())), preferred_element_type=F32)
        residual = loads_ref[:, columns] + fold(y[: 3 * block], 3)
        residual_ref[:, columns] = residual
        extra = y[3 * block + 48 : 3 * block + 64]
        weight = extra[0:1]
        weight_ref[:, columns] = weight
        weighted_ref[:, columns] = residual * weight
        inverse_ref[:, columns] = (extra[1:2] * 256.0 + extra[2:3]).astype(jnp.int32)
        own_reach = jnp.concatenate([weight * basis_ref[:, columns], jnp.zeros((12, tile), F32)], axis=0)
        near = fold(y[3 * block : 3 * block + 48], 3)
        put_terms(reach_ref, 0, columns, two_terms(jnp.concatenate([own_reach, near], axis=0)))

    over_columns(width, 12, one)
    coarse = lax.dot_general(
        weighted_ref[...], basis_ref[...], (((1,), (1,)), ((), ())), precision=HIGH, preferred_element_type=F32
    )
    coarse_ref[...] = place(coarse, table_ref, range(4), coarse_ref.shape[1])


def first_sweep(begin, *refs):
    if begin:
        relax_ref, weighted_ref, matrix_ref, solve_ref, terms_ref = refs
        solve_ref[...] = relax_ref[0, 0] * weighted_ref[...]
    else:
        relax_ref, weighted_ref, matrix_ref, old_ref, solve_ref, terms_ref = refs
        solve_ref[...] = old_ref[...]
    sweep(weighted_ref, solve_ref, terms_ref, relax_ref[0, 0], matrix_ref)


def first_correct(
    table_ref, solve_ref, coarse_ref, coarse_inverse_ref, basis_ref, weight_ref, rows_ref,
    own_ref, coarse_solution_ref, o0, o1, o2, o3, terms_ref, hold_ref,
):
    coarse_solution = dot(coarse_ref[...], coarse_inverse_ref[...])
    coarse_solution_ref[...] = coarse_solution
    own_ref[...] = correct(solve_ref, coarse_solution, table_ref, basis_ref, weight_ref)
    gather_slots(own_ref[...], terms_ref, rows_ref, table_ref, hold_ref, (o0, o1, o2, o3))


def settle(first, start, *refs):
    refs = list(refs)
    solve_ref, weighted_ref, coarse_solution_ref, coarse_ref = refs[:4]
    rest = refs[4:]
    if start:
        rho_ref, coarse_rho_ref, left_ref, right_ref = rest
    elif first:
        precond_ref, step_ref, rho_ref, coarse_rho_ref, direction_ref, direction_terms_ref, solution_ref, left_ref, right_ref = rest
    else:
        precond_ref, step_ref, back_ref, old_direction_ref, old_solution_ref = rest[:5]
        rho_ref, coarse_rho_ref, direction_ref, direction_terms_ref, solution_ref, left_ref, right_ref = rest[5:]
    put_terms(left_ref, 0, slice(None), three_terms(solve_ref[...]))
    put_terms(right_ref, 0, slice(None), three_terms(weighted_ref[...]))
    rho_ref[...] = gram(left_ref[...], right_ref[...], 3, 3)
    coarse_rho_ref[...] = lax.dot_general(
        coarse_solution_ref[...], coarse_ref[...], (((1,), (1,)), ((), ())), precision=HIGH, preferred_element_type=F32
    )
    if start:
        return
    step = stacked(step_ref[...])
    back = None if first else stacked(back_ref[...])

    def one(columns, start_at, tile):
        direction = precond_ref[:, columns]
        if not first:
            direction = direction + mix(back, old_direction_ref[:, columns])
        direction_ref[:, columns] = direction
        put_terms(direction_terms_ref, 0, columns, three_terms(direction))
        moved = mix(step, direction)
        solution_ref[:, columns] = moved if first else old_solution_ref[:, columns] + moved

    over_columns(solve_ref.shape[1], 4, one)


def apply_matrix(first, *refs):
    refs = list(refs)
    table_ref, own_ref, rho_ref, matrix_ref, reach_ref, inverse_ref = refs[:6]
    ins, rest = refs[6:10], refs[10:]
    direction_terms_ref = None if first else rest.pop(0)
    precond_ref, partial_ref, sums_ref, terms_ref, more_ref = rest
    block = own_ref.shape[0]

    def gain(columns, y):
        precond_ref[:, columns] = own_ref[:, columns] + y

    scatter_faces(ins, terms_ref, inverse_ref, table_ref, gain)
    put_terms(terms_ref, 0, slice(None), three_terms(precond_ref[...]))
    put_terms(more_ref, 0, slice(None), two_terms(precond_ref[...]))

    def emit(columns, y):
        partial_ref[:, columns] = y

    product(more_ref.at[0 : 2 * block], matrix_ref, emit)
    put_terms(more_ref, 0, slice(None), three_terms(partial_ref[...]))
    partial = more_ref[...]
    sums_ref[:, 0:PLACE] = jnp.zeros((block, PLACE), F32)
    sums_ref[:, 0:block] = rho_ref[...]
    sums_ref[:, block : 2 * block] = gram(partial, terms_ref[...], 3, 3)
    if not first:
        sums_ref[:, 2 * block : 3 * block] = gram(partial, direction_terms_ref[...], 3, 3)
    coarse = gram(partial, reach_ref[...], 3, 2)
    members = (0, 1, 2, 3) + tuple(range(16, 32))
    sums_ref[:, PLACE:] = place(coarse, table_ref, members, sums_ref.shape[1] - PLACE)


def gather_image(table_ref, partial_ref, rows_ref, o0, o1, o2, o3, terms_ref, hold_ref):
    gather_slots(partial_ref[...], terms_ref, rows_ref, table_ref, hold_ref, (o0, o1, o2, o3))


def scatter_image(table_ref, partial_ref, inverse_ref, i0, i1, i2, i3, image_ref, terms_ref):
    def gain(columns, y):
        image_ref[:, columns] = partial_ref[:, columns] + y

    scatter_faces((i0, i1, i2, i3), terms_ref, inverse_ref, table_ref, gain)


def invert(rho_ref, inverse_ref):
    n = rho_ref.shape[0]
    row = lax.broadcasted_iota(jnp.int32, (n, n), 0)
    one = (row == lax.broadcasted_iota(jnp.int32, (n, n), 1)).astype(F32)
    inverse_ref[...] = spd_solve(rho_ref[...], one)


def advance(first, last, *refs):
    refs = list(refs)
    sums_ref, coarse_rho_ref, image_part_ref, residual_ref = refs[:4]
    rest = refs[4:]
    if not first:
        old_image_ref, old_curvature_ref, old_rho_inverse_ref = rest[:3]
        rest = rest[3:]
    if last:
        precond_ref, old_direction_ref, old_solution_ref, new_solution_ref, new_residual_ref = rest
    else:
        if not first:
            old_coarse_image_ref = rest.pop(0)
        table_ref, relax_ref, matrix_ref, weight_ref, basis_ref, rows_ref, coarse_ref, coarse_inverse_ref = rest[:8]
        rest = rest[8:]
        new_residual_ref, image_ref, curvature_ref, rho_out_ref, step_ref = rest[:5]
        rest = rest[5:]
        if not first:
            back_ref = rest.pop(0)
        coarse_image_ref, new_coarse_ref, coarse_solution_ref, solve_ref, weighted_ref, own_ref = rest[:6]
        o0, o1, o2, o3, terms_ref, hold_ref = rest[6:]
    block, width = residual_ref.shape
    rho = symmetric(sums_ref[:, 0:block] + coarse_rho_ref[...])
    curvature = symmetric(sums_ref[:, block : 2 * block])
    if not first:
        beta = dot(old_rho_inverse_ref[...], rho)
        back = beta.T
        cross = dot(sums_ref[:, 2 * block : 3 * block], beta)
        curvature = curvature + (cross + cross.T) + symmetric(dot(back, dot(old_curvature_ref[...], beta)))
        back_stack = stacked(back)
    step = spd_solve(curvature, rho).T
    step_stack = stacked(step)

    def one(columns, start, tile):
        image = image_part_ref[:, columns]
        if not first:
            image = image + mix(back_stack, old_image_ref[:, columns])
        residual = residual_ref[:, columns] - mix(step_stack, image)
        new_residual_ref[:, columns] = residual
        if last:
            direction = precond_ref[:, columns] + mix(back_stack, old_direction_ref[:, columns])
            new_solution_ref[:, columns] = old_solution_ref[:, columns] + mix(step_stack, direction)
        else:
            image_ref[:, columns] = image
            weighted = residual * weight_ref[:, columns]
            weighted_ref[:, columns] = weighted
            solve_ref[:, columns] = relax_ref[0, 0] * weighted

    over_columns(width, 4, one)
    if last:
        return
    step_ref[...] = step
    curvature_ref[...] = curvature
    rho_out_ref[...] = rho
    coarse_image = sums_ref[:, PLACE:]
    if not first:
        back_ref[...] = back
        coarse_image = coarse_image + dot(back, old_coarse_image_ref[...])
    coarse_image_ref[...] = coarse_image
    coarse = coarse_ref[...] - dot(step, coarse_image)
    new_coarse_ref[...] = coarse
    coarse_solution = dot(coarse, coarse_inverse_ref[...])
    coarse_solution_ref[...] = coarse_solution

    def again(t, carry):
        sweep(weighted_ref, solve_ref, terms_ref.at[0 : 2 * block], relax_ref[0, 0], matrix_ref)
        return carry

    lax.fori_loop(0, DEG, again, 0)
    own_ref[...] = correct(solve_ref, coarse_solution, table_ref, basis_ref, weight_ref)
    gather_slots(own_ref[...], terms_ref, rows_ref, table_ref, hold_ref, (o0, o1, o2, o3))


def on_core(kernel, args, scalars, outs, scratch, flops, limit=12 * MIB):
    specs = [pl.BlockSpec(memory_space=pltpu.SMEM if at in scalars else pltpu.VMEM) for at in range(len(args))]
    size = sum(x.size * x.dtype.itemsize for x in args) + sum(4 * o.size for o in outs)
    return pl.pallas_call(
        kernel,
        out_shape=outs,
        in_specs=specs,
        out_specs=[pl.BlockSpec(memory_space=pltpu.VMEM)] * len(outs),
        scratch_shapes=scratch,
        compiler_params=pltpu.CompilerParams(vmem_limit_bytes=limit),
        cost_estimate=pl.CostEstimate(flops=flops, bytes_accessed=size, transcendentals=0),
    )(*args)


def swap(x, axis, partner):
    return lax.ppermute(x, axis, [(i, partner(i)) for i in range(lax.axis_size(axis))])


def exchange(slots):
    subs, segs = lax.axis_size("sub"), lax.axis_size("seg")
    inner = [(i, ((i - 1) ^ 1) + 1) for i in range(1, segs - 1)]
    return [
        swap(slots[0], "sub", lambda i: i ^ 1),
        swap(slots[1], "sub", lambda i: (((i - 1) % subs ^ 1) + 1) % subs),
        swap(slots[2], "seg", lambda i: i ^ 1),
        lax.ppermute(slots[3], "seg", inner),
    ]


def pair_sum(x):
    return x + swap(x, "seg", lambda i: i ^ 1)


def ring_swaps(x, axis, stride):
    return [swap(x, axis, lambda i, k=k: i ^ (k * stride)) for k in (1, 2, 3)]


def beside(work, *others):
    return lax.optimization_barrier((work, *others))


def add_all(x, parts):
    return (x + parts[0]) + (parts[1] + parts[2])


def body(nodal_loads, schur_matrix, face_rows, face_len, relax_step, coarse_basis, primal_index, coarse_inverse):
    s, j = lax.axis_index("seg"), lax.axis_index("sub")
    segs, subs = lax.axis_size("seg"), lax.axis_size("sub")
    loads, matrix, rows, basis = nodal_loads[0, 0], schur_matrix[0, 0], face_rows[0], coarse_basis[0, 0]
    block, width = loads.shape
    face_width = width // 4
    coarse_count = coarse_inverse.shape[0]
    left, right = (j + subs - 1) % subs, (j + 1) % subs
    down, up = jnp.maximum(s - 1, 0), jnp.minimum(s + 1, segs - 1)
    sub_odd, seg_odd = j % 2, s % 2
    faces_of = jnp.stack([1 - sub_odd, sub_odd, 3 - seg_odd, 2 + seg_odd])
    seg_of = jnp.where(faces_of == 2, down, s)
    sub_of = jnp.where(faces_of == 0, left, j)
    flat = (seg_of * subs + sub_of) * 2 + (faces_of >= 2).astype(jnp.int32)
    there = jnp.where(faces_of == 2, s > 0, jnp.where(faces_of == 3, s < segs - 1, True))
    lengths = jnp.where(there, jnp.take(face_len.reshape(-1), flat, mode="clip"), 0)
    here = s * subs + j
    cell = jnp.stack([here, here, here, here, s * subs + left, s * subs + right, down * subs + j, up * subs + j])
    index = jnp.take(primal_index.reshape(segs * subs, 4), cell, axis=0, mode="clip").reshape(-1)
    table = jnp.concatenate([lengths, faces_of, index])

    shape = lambda *size: jax.ShapeDtypeStruct(size, F32)
    full, small, coarse_block = shape(block, width), shape(block, block), shape(block, coarse_count)
    terms = pltpu.VMEM((3 * block, width), BF16)
    hold = pltpu.VMEM((block, width), F32)
    faces = [shape(block, face_width)] * 4
    move = 2 * 3 * block * width * width
    turn = 2 * 2 * block * width * width
    light = 2 * 9 * block * block * width

    wide = [shape(block + 8, face_width)] * 4
    slots = on_core(
        first_gather, (table, loads, basis, rows), (0,), wide,
        [pltpu.VMEM((3 * (block + 16), width), BF16), pltpu.VMEM((block + 16, width), F32)], move,
    )
    got = exchange(slots)
    residual, weighted, reach, weight, inverse, coarse = on_core(
        first_scatter, (table, loads, basis, rows, *got), (0,),
        [full, full, jax.ShapeDtypeStruct((64, width), BF16), shape(1, width),
         jax.ShapeDtypeStruct((1, width), jnp.int32), coarse_block],
        [pltpu.VMEM((3 * block + 64, width), BF16)], move,
    )
    half_terms = pltpu.VMEM((2 * block, width), BF16)

    def one_sweep(*old):
        return on_core(
            functools.partial(first_sweep, not old), (relax_step, weighted, matrix, *old), (0,), [full], [half_terms], turn,
        )[0]

    coarse = pair_sum(coarse)
    for axis, stride in (("seg", 2), ("sub", 1), ("sub", 4)):
        parts = ring_swaps(coarse, axis, stride)
        solve = one_sweep() if axis == "seg" else one_sweep(solve)
        solve, *parts = beside(solve, *parts)
        coarse = add_all(coarse, parts)
    own, coarse_solution, *slots = on_core(
        first_correct, (table, solve, coarse, coarse_inverse, basis, weight, rows), (0,),
        [full, coarse_block, *faces], [terms, hold], move,
    )
    three = jax.ShapeDtypeStruct((3 * block, width), BF16)
    step = back = precond = direction = image = answer = curvature = rho = coarse_image = None
    for iteration in range(ITERS):
        first, last = iteration == 0, iteration + 1 == ITERS
        got = exchange(slots)
        settled = [solve, weighted, coarse_solution, coarse]
        outs = [small, small]
        if iteration:
            settled += [precond, step] + ([back, direction, answer] if iteration > 1 else [])
            outs += [full, three, full]
        settled = on_core(
            functools.partial(settle, iteration == 1, first), settled, (), outs, [terms, terms], light,
        )
        got = list(beside(settled[0], *got))
        local_rho, coarse_rho = got.pop(0), settled[1]
        if iteration:
            direction, direction_terms, answer = settled[2:]
        precond, partial, sums = on_core(
            functools.partial(apply_matrix, first),
            (table, own, local_rho, matrix, reach, inverse, *got, *(() if first else (direction_terms,))), (0,),
            [full, full, shape(block, PLACE + coarse_count)], [terms, terms], turn + move,
        )
        part = swap(sums, "seg", lambda i: i ^ 1)
        slots = on_core(gather_image, (table, partial, rows), (0,), faces, [terms, hold], move)
        part, *slots = beside(part, *slots)
        sums = sums + part
        parts = ring_swaps(sums, "seg", 2)
        got = exchange(slots)
        sums = add_all(sums, parts)
        sums, *got = beside(sums, *got)
        parts = ring_swaps(sums, "sub", 1)
        image_part, = on_core(scatter_image, (table, partial, inverse, *got), (0,), [full], [terms], move)
        image_part, *parts = beside(image_part, *parts)
        sums = add_all(sums, parts)
        parts = ring_swaps(sums, "sub", 4)
        args = [coarse_rho, image_part, residual]
        if not first:
            rho_inverse, = on_core(invert, (rho,), (), [small], [], light)
            rho_inverse, *parts = beside(rho_inverse, *parts)
            args += [image, curvature, rho_inverse]
        args = [add_all(sums, parts), *args]
        if last:
            answer, residual = on_core(
                functools.partial(advance, first, last), (*args, precond, direction, answer), (), [full, full], [], light,
            )
            break
        if not first:
            args += [coarse_image]
        at = len(args)
        args += [table, relax_step, matrix, weight, basis, rows, coarse, coarse_inverse]
        outs = [full, full, small, small, small] + ([] if first else [small])
        outs += [coarse_block, coarse_block, coarse_block, full, full, full, *faces]
        residual, image, curvature, rho, step, *rest = on_core(
            functools.partial(advance, first, last), args, (at, at + 1), outs, [terms, hold], 3 * turn + move,
        )
        if not first:
            back = rest.pop(0)
        coarse_image, coarse, coarse_solution, solve, weighted, own, *slots = rest
    return (answer[None, None], residual[None, None])


def solution(mesh):
    placed = (
        P("seg", "sub", None, None),
        P("seg", "sub", None, None),
        P("seg", "sub", None),
        P(),
        P("seg", "sub"),
        P("seg", "sub", None, None),
        P(),
        P(),
    )
    return jax.shard_map(
        body,
        mesh=mesh,
        in_specs=placed,
        out_specs=(P("seg", "sub", None, None), P("seg", "sub", None, None)),
        check_vma=False,
    )
```

```python
import functools

import jax
import jax.numpy as jnp
from jax import lax
from jax.experimental import pallas as pl
from jax.experimental.pallas import tpu as pltpu
from jax.sharding import PartitionSpec as P

DEG = 3
ITERS = 3
HIGH = lax.Precision.HIGHEST
F32 = jnp.float32
BF16 = jnp.bfloat16
MIB = 1 << 20

PLACE = 128
FACE = 4
INDEX = 8


def dot(a, b):
    return jnp.dot(a, b, precision=HIGH, preferred_element_type=F32)


def symmetric(matrix):
    return 0.5 * (matrix + matrix.T)


def two_terms(x):
    hi = x.astype(BF16)
    return hi, (x - hi.astype(F32)).astype(BF16)


def three_terms(x):
    hi = x.astype(BF16)
    rest = x - hi.astype(F32)
    mid = rest.astype(BF16)
    return hi, mid, (rest - mid.astype(F32)).astype(BF16)


def put_terms(ref, first, columns, terms):
    rows = terms[0].shape[0]
    for at, term in enumerate(terms):
        ref[first + at * rows : first + (at + 1) * rows, columns] = term


def fold(y, parts):
    rows = y.shape[0] // parts
    total = y[:rows]
    for at in range(1, parts):
        total = total + y[at * rows : (at + 1) * rows]
    return total


def gram(left, right, left_parts, right_parts):
    y = lax.dot_general(left, right, (((1,), (1,)), ((), ())), preferred_element_type=F32)
    y = fold(y, left_parts)
    columns = y.shape[1] // right_parts
    total = y[:, :columns]
    for at in range(1, right_parts):
        total = total + y[:, at * columns : (at + 1) * columns]
    return total


def stacked(matrix):
    return jnp.concatenate([jnp.concatenate([term] * 3, axis=1) for term in three_terms(matrix)], axis=0)


def mix(stack, x):
    terms = jnp.concatenate(three_terms(x), axis=0)
    return fold(jnp.dot(stack, terms, preferred_element_type=F32), 3)


def cut(width, parts):
    return width // parts if width % parts == 0 and (width // parts) % 128 == 0 else width // 4


def over_columns(width, parts, one):
    tile = cut(width, parts)

    def step(t, carry):
        start = pl.multiple_of(t * tile, tile)
        one(pl.ds(start, tile), start, tile)
        return carry

    lax.fori_loop(0, width // tile, step, 0)


def spd_solve(a, b):
    n = a.shape[0]
    both = jnp.concatenate([a, b], axis=1)
    row = lax.broadcasted_iota(jnp.int32, (n, 1), 0)
    for k in range(0, n, 2):
        upper, lower = both[k : k + 1, :], both[k + 1 : k + 2, :]
        first, second = both[:, k : k + 1], both[:, k + 1 : k + 2]
        over = 1.0 / upper[:, k : k + 1]
        right = upper[:, k + 1 : k + 2] * over
        down = lower[:, k : k + 1]
        rest = lower[:, k + 1 : k + 2] - down * right
        upper = upper * over
        lower = (lower - down * upper) / rest
        upper = upper - right * lower
        both = jnp.where(row == k, upper, jnp.where(row == k + 1, lower, both - first * upper - second * lower))
    return both[:, n:]


def one_hot(index, chunk, within):
    low = jnp.where(index // 256 == chunk, (index % 256).astype(F32), -1.0).astype(BF16)
    return jnp.where(within == low, jnp.ones((), BF16), jnp.zeros((), BF16))


def within_chunk(columns):
    return lax.broadcasted_iota(jnp.int32, (256, columns), 0).astype(F32).astype(BF16)


def permute(terms_ref, index_ref, chunks, emit):
    within = within_chunk(cut(index_ref.shape[1], 4))

    def one(columns, start, tile):
        index = index_ref[0:1, columns]
        y = None
        for at, chunk in enumerate(chunks):
            hot = one_hot(index, chunk, within)
            part = jnp.dot(terms_ref[:, at * 256 : (at + 1) * 256], hot, preferred_element_type=F32)
            y = part if y is None else y + part
        emit(columns, fold(y, 3))

    over_columns(index_ref.shape[1], 4, one)


def face_columns(table_ref, swap, face_width):
    return pl.ds(pl.multiple_of(table_ref[FACE + swap] * face_width, face_width), face_width)


def gather_slots(x, terms_ref, rows_ref, table_ref, hold_ref, out_refs):
    put_terms(terms_ref, 0, slice(None), three_terms(x))

    def emit(columns, y):
        hold_ref[:, columns] = y

    permute(terms_ref, rows_ref, range(rows_ref.shape[1] // 256), emit)
    face_width = rows_ref.shape[1] // 4
    at = lax.broadcasted_iota(jnp.int32, (1, face_width), 1)
    for swap, out in enumerate(out_refs):
        part = hold_ref[0 : out.shape[0], face_columns(table_ref, swap, face_width)]
        out[...] = part * (at < table_ref[swap]).astype(F32)


def face_chunks(swaps, table_ref, face_width):
    each = face_width // 256
    return [table_ref[FACE + swap] * each + part for swap in swaps for part in range(each)]


def scatter_faces(in_refs, swaps, terms_ref, inverse_ref, table_ref, emit):
    face_width = inverse_ref.shape[1] // 4
    for at, ref in enumerate(in_refs):
        put_terms(terms_ref, 0, slice(at * face_width, (at + 1) * face_width), three_terms(ref[...]))
    permute(terms_ref, inverse_ref, face_chunks(swaps, table_ref, face_width), emit)


def product(terms_ref, matrix_ref, emit):
    def one(columns, start, tile):
        emit(columns, fold(jnp.dot(terms_ref[...], matrix_ref[:, columns], preferred_element_type=F32), 2))

    over_columns(matrix_ref.shape[1], 3, one)


def sweep(weighted_ref, solve_ref, terms_ref, relax, matrix_ref):
    put_terms(terms_ref, 0, slice(None), two_terms(solve_ref[...]))

    def emit(columns, y):
        solve_ref[:, columns] = relax * weighted_ref[:, columns] + solve_ref[:, columns] - relax * y

    product(terms_ref, matrix_ref, emit)


def place(columns, table_ref, members, width):
    at = lax.broadcasted_iota(jnp.int32, (1, width), 1)
    total = jnp.zeros((columns.shape[0], width), F32)
    for member in members:
        total = total + columns[:, member : member + 1] * (at == table_ref[INDEX + member]).astype(F32)
    return total


def correct(solve_ref, coarse_solution, table_ref, basis_ref, weight_ref):
    at = lax.broadcasted_iota(jnp.int32, (1, coarse_solution.shape[1]), 1)
    solve = solve_ref[...]
    for face in range(4):
        mine = (at == table_ref[INDEX + face]).astype(F32)
        picked = jnp.sum(coarse_solution * mine, axis=1, keepdims=True)
        solve = solve + picked * basis_ref[face : face + 1, :]
    return solve * weight_ref[...]


def fill_table(table_ref, face_len_ref, primal_ref):
    s, j = lax.axis_index("seg"), lax.axis_index("sub")
    segs, subs = face_len_ref.shape[:2]
    left, right = lax.rem(j + subs - 1, subs), lax.rem(j + 1, subs)
    down, up = jnp.maximum(s - 1, 0), jnp.minimum(s + 1, segs - 1)
    sub_odd, seg_odd = lax.rem(j, 2), lax.rem(s, 2)
    lengths = (
        face_len_ref[s, left, 0],
        face_len_ref[s, j, 0],
        jnp.where(s > 0, face_len_ref[down, j, 1], 0),
        jnp.where(s < segs - 1, face_len_ref[s, j, 1], 0),
    )
    table_ref[0] = jnp.where(sub_odd == 0, lengths[1], lengths[0])
    table_ref[1] = jnp.where(sub_odd == 0, lengths[0], lengths[1])
    table_ref[2] = jnp.where(seg_odd == 0, lengths[3], lengths[2])
    table_ref[3] = jnp.where(seg_odd == 0, lengths[2], lengths[3])
    table_ref[FACE] = 1 - sub_odd
    table_ref[FACE + 1] = sub_odd
    table_ref[FACE + 2] = 3 - seg_odd
    table_ref[FACE + 3] = 2 + seg_odd
    for at, (row, column) in enumerate(((s, j), (s, left), (s, right), (down, j), (up, j))):
        first = INDEX if at == 0 else INDEX + 12 + 4 * at
        for face in range(4):
            table_ref[first + face] = primal_ref[row, column, face]


def first_gather(
    face_len_ref, primal_ref, loads_ref, basis_ref, rows_ref, table_ref, o0, o1, o2, o3, terms_ref, hold_ref
):
    fill_table(table_ref, face_len_ref, primal_ref)
    spare = jnp.zeros((12, loads_ref.shape[1]), F32)
    x = jnp.concatenate([loads_ref[...], 0.5 * basis_ref[...], spare], axis=0)
    gather_slots(x, terms_ref, rows_ref, table_ref, hold_ref, (o0, o1, o2, o3))


def prepare(table_ref, rows_ref, matrix_at, weight_ref, inverse_ref, matrix_ref, terms_ref, sem):
    copy = pltpu.make_async_copy(matrix_at, matrix_ref, sem)
    copy.start()
    width = rows_ref.shape[1]
    face_width = width // 4
    row = lax.broadcasted_iota(jnp.int32, (16, face_width), 0)
    column = lax.broadcasted_iota(jnp.int32, (16, face_width), 1)
    for swap in range(4):
        slot = column + table_ref[FACE + swap] * face_width
        weight = 1.0 - 0.5 * (column < table_ref[swap]).astype(F32)
        extra = jnp.where(
            row == 0,
            weight,
            jnp.where(row == 1, (slot // 256).astype(F32), jnp.where(row == 2, (slot % 256).astype(F32), 0.0)),
        )
        terms_ref[:, face_columns(table_ref, swap, face_width)] = extra.astype(BF16)
    within = within_chunk(width)

    def one(chunk, carry):
        columns = pl.ds(pl.multiple_of(chunk * 256, 256), 256)
        hot = one_hot(rows_ref[...], chunk, within)
        y = lax.dot_general(terms_ref[...], hot, (((1,), (1,)), ((), ())), preferred_element_type=F32)
        weight_ref[:, columns] = y[0:1]
        inverse_ref[:, columns] = (y[1:2] * 256.0 + y[2:3]).astype(jnp.int32)
        return carry

    lax.fori_loop(0, width // 256, one, 0)
    copy.wait()


def first_scatter(
    table_ref, loads_ref, basis_ref, weight_ref, inverse_ref, i0, i1, i2, i3,
    residual_ref, weighted_ref, reach_ref, coarse_ref, terms_ref,
):
    block, width = loads_ref.shape
    face_width = width // 4
    row = lax.broadcasted_iota(jnp.int32, (16, face_width), 0)
    for swap, ref in enumerate((i0, i1, i2, i3)):
        face = table_ref[FACE + swap]
        got = ref[block : block + 4, :]
        spread = jnp.where(row // 4 == face, jnp.concatenate([got] * 4, axis=0), 0.0)
        both = jnp.concatenate([ref[0:block, :], spread], axis=0)
        put_terms(terms_ref, 0, slice(swap * face_width, (swap + 1) * face_width), three_terms(both))

    def gain(columns, y):
        residual = loads_ref[:, columns] + y[:block]
        weight = weight_ref[:, columns]
        residual_ref[:, columns] = residual
        weighted_ref[:, columns] = residual * weight
        blank = jnp.zeros((12, y.shape[1]), F32)
        reach = jnp.concatenate([weight * basis_ref[:, columns], blank, y[block:]], axis=0)
        put_terms(reach_ref, 0, columns, two_terms(reach))

    permute(terms_ref, inverse_ref, face_chunks(range(4), table_ref, face_width), gain)
    coarse = lax.dot_general(
        weighted_ref[...], basis_ref[...], (((1,), (1,)), ((), ())), precision=HIGH, preferred_element_type=F32
    )
    coarse_ref[...] = place(coarse, table_ref, range(4), coarse_ref.shape[1])


def first_sweep(begin, *refs):
    if begin:
        relax_ref, weighted_ref, matrix_ref, solve_ref, terms_ref = refs
        solve_ref[...] = relax_ref[0, 0] * weighted_ref[...]
    else:
        relax_ref, weighted_ref, matrix_ref, old_ref, solve_ref, terms_ref = refs
        solve_ref[...] = old_ref[...]
    sweep(weighted_ref, solve_ref, terms_ref, relax_ref[0, 0], matrix_ref)


def first_correct(
    table_ref, solve_ref, coarse_ref, coarse_inverse_ref, basis_ref, weight_ref, rows_ref,
    own_ref, coarse_solution_ref, o0, o1, o2, o3, terms_ref, hold_ref,
):
    coarse_solution = dot(coarse_ref[...], coarse_inverse_ref[...])
    coarse_solution_ref[...] = coarse_solution
    own_ref[...] = correct(solve_ref, coarse_solution, table_ref, basis_ref, weight_ref)
    gather_slots(own_ref[...], terms_ref, rows_ref, table_ref, hold_ref, (o0, o1, o2, o3))


def settle(first, start, *refs):
    refs = list(refs)
    solve_ref, weighted_ref, coarse_solution_ref, coarse_ref = refs[:4]
    rest = refs[4:]
    if start:
        rho_ref, coarse_rho_ref, left_ref, right_ref = rest
    else:
        precond_ref, step_ref = rest[:2]
        rest = rest[2:]
        if not first:
            back_ref, old_direction_ref, old_solution_ref = rest[:3]
            rest = rest[3:]
        rho_ref, coarse_rho_ref, direction_ref, direction_terms_ref, solution_ref, left_ref, right_ref = rest
    put_terms(left_ref, 0, slice(None), three_terms(solve_ref[...]))
    put_terms(right_ref, 0, slice(None), three_terms(weighted_ref[...]))
    rho_ref[...] = gram(left_ref[...], right_ref[...], 3, 3)
    coarse_rho_ref[...] = lax.dot_general(
        coarse_solution_ref[...], coarse_ref[...], (((1,), (1,)), ((), ())), precision=HIGH, preferred_element_type=F32
    )
    if start:
        return
    step = stacked(step_ref[...])
    back = None if first else stacked(back_ref[...])

    def turn(columns, start_at, tile):
        direction = precond_ref[:, columns]
        if not first:
            direction = direction + mix(back, old_direction_ref[:, columns])
        direction_ref[:, columns] = direction
        put_terms(direction_terms_ref, 0, columns, three_terms(direction))
        moved = mix(step, direction)
        solution_ref[:, columns] = moved if first else old_solution_ref[:, columns] + moved

    over_columns(solve_ref.shape[1], 4, turn)


def apply_matrix(first, *refs):
    refs = list(refs)
    table_ref, own_ref, rho_ref, matrix_ref, reach_ref, inverse_ref = refs[:6]
    ins, rest = refs[6:8], refs[8:]
    direction_terms_ref = None if first else rest.pop(0)
    precond_ref, partial_ref, sums_ref, terms_ref, more_ref = rest
    block = own_ref.shape[0]

    def gain(columns, y):
        precond_ref[:, columns] = own_ref[:, columns] + y

    scatter_faces(ins, (0, 1), terms_ref, inverse_ref, table_ref, gain)
    put_terms(terms_ref, 0, slice(None), three_terms(precond_ref[...]))
    put_terms(more_ref, 0, slice(None), two_terms(precond_ref[...]))

    def emit(columns, y):
        partial_ref[:, columns] = y

    product(more_ref.at[0 : 2 * block], matrix_ref, emit)
    put_terms(more_ref, 0, slice(None), three_terms(partial_ref[...]))
    partial = more_ref[...]
    sums_ref[:, 0:PLACE] = jnp.zeros((block, PLACE), F32)
    sums_ref[:, 0:block] = rho_ref[...]
    sums_ref[:, block : 2 * block] = gram(partial, terms_ref[...], 3, 3)
    if not first:
        sums_ref[:, 2 * block : 3 * block] = gram(partial, direction_terms_ref[...], 3, 3)
    coarse = gram(partial, reach_ref[...], 3, 2)
    members = (0, 1, 2, 3) + tuple(range(16, 32))
    sums_ref[:, PLACE:] = place(coarse, table_ref, members, sums_ref.shape[1] - PLACE)


def gather_image(table_ref, partial_ref, rows_ref, o0, o1, o2, o3, terms_ref, hold_ref):
    gather_slots(partial_ref[...], terms_ref, rows_ref, table_ref, hold_ref, (o0, o1, o2, o3))


def add_faces(swaps, table_ref, block_ref, inverse_ref, i0, i1, sum_ref, terms_ref):
    def gain(columns, y):
        sum_ref[:, columns] = block_ref[:, columns] + y

    scatter_faces((i0, i1), swaps, terms_ref, inverse_ref, table_ref, gain)


def invert(rho_ref, inverse_ref):
    n = rho_ref.shape[0]
    row = lax.broadcasted_iota(jnp.int32, (n, n), 0)
    one = (row == lax.broadcasted_iota(jnp.int32, (n, n), 1)).astype(F32)
    inverse_ref[...] = spd_solve(rho_ref[...], one)


def advance(first, last, *refs):
    refs = list(refs)
    sums_ref, coarse_rho_ref, image_part_ref, residual_ref = refs[:4]
    rest = refs[4:]
    if not first:
        old_image_ref, old_curvature_ref, old_rho_inverse_ref = rest[:3]
        rest = rest[3:]
    if last:
        precond_ref, old_direction_ref, old_solution_ref, new_solution_ref, new_residual_ref = rest
    else:
        if not first:
            old_coarse_image_ref = rest.pop(0)
        table_ref, relax_ref, matrix_ref, weight_ref, basis_ref, rows_ref, coarse_ref, coarse_inverse_ref = rest[:8]
        rest = rest[8:]
        new_residual_ref, image_ref, curvature_ref, rho_out_ref, step_ref = rest[:5]
        rest = rest[5:]
        if not first:
            back_ref = rest.pop(0)
        coarse_image_ref, new_coarse_ref, coarse_solution_ref, solve_ref, weighted_ref, own_ref = rest[:6]
        o0, o1, o2, o3, terms_ref, hold_ref = rest[6:]
    block, width = residual_ref.shape
    rho = symmetric(sums_ref[:, 0:block] + coarse_rho_ref[...])
    curvature = symmetric(sums_ref[:, block : 2 * block])
    if not first:
        beta = dot(old_rho_inverse_ref[...], rho)
        back = beta.T
        cross = dot(sums_ref[:, 2 * block : 3 * block], beta)
        curvature = curvature + (cross + cross.T) + symmetric(dot(back, dot(old_curvature_ref[...], beta)))
        back_stack = stacked(back)
    step = spd_solve(curvature, rho).T
    step_stack = stacked(step)

    def one(columns, start, tile):
        image = image_part_ref[:, columns]
        if not first:
            image = image + mix(back_stack, old_image_ref[:, columns])
        residual = residual_ref[:, columns] - mix(step_stack, image)
        new_residual_ref[:, columns] = residual
        if last:
            direction = precond_ref[:, columns] + mix(back_stack, old_direction_ref[:, columns])
            new_solution_ref[:, columns] = old_solution_ref[:, columns] + mix(step_stack, direction)
        else:
            image_ref[:, columns] = image
            weighted = residual * weight_ref[:, columns]
            weighted_ref[:, columns] = weighted
            solve_ref[:, columns] = relax_ref[0, 0] * weighted

    over_columns(width, 4, one)
    if last:
        return
    step_ref[...] = step
    curvature_ref[...] = curvature
    rho_out_ref[...] = rho
    coarse_image = sums_ref[:, PLACE:]
    if not first:
        back_ref[...] = back
        coarse_image = coarse_image + dot(back, old_coarse_image_ref[...])
    coarse_image_ref[...] = coarse_image
    coarse = coarse_ref[...] - dot(step, coarse_image)
    new_coarse_ref[...] = coarse
    coarse_solution = dot(coarse, coarse_inverse_ref[...])
    coarse_solution_ref[...] = coarse_solution

    def again(t, carry):
        sweep(weighted_ref, solve_ref, terms_ref.at[0 : 2 * block], relax_ref[0, 0], matrix_ref)
        return carry

    lax.fori_loop(0, DEG, again, 0)
    own_ref[...] = correct(solve_ref, coarse_solution, table_ref, basis_ref, weight_ref)
    gather_slots(own_ref[...], terms_ref, rows_ref, table_ref, hold_ref, (o0, o1, o2, o3))


def on_core(kernel, args, scalars, outs, scratch, flops, far=(), scalar_outs=(), limit=12 * MIB):
    def spec(at, scalar, far):
        return pl.BlockSpec(memory_space=pltpu.SMEM if at in scalar else pltpu.HBM if at in far else pltpu.VMEM)

    size = sum(x.size * x.dtype.itemsize for x in args) + sum(4 * o.size for o in outs)
    return pl.pallas_call(
        kernel,
        out_shape=outs,
        in_specs=[spec(at, scalars, far) for at in range(len(args))],
        out_specs=[spec(at, scalar_outs, ()) for at in range(len(outs))],
        scratch_shapes=scratch,
        compiler_params=pltpu.CompilerParams(vmem_limit_bytes=limit),
        cost_estimate=pl.CostEstimate(flops=flops, bytes_accessed=size, transcendentals=0),
    )(*args)


def swap(x, axis, partner):
    return lax.ppermute(x, axis, [(i, partner(i)) for i in range(lax.axis_size(axis))])


def exchange(slots):
    subs, segs = lax.axis_size("sub"), lax.axis_size("seg")
    inner = [(i, ((i - 1) ^ 1) + 1) for i in range(1, segs - 1)]
    return [
        swap(slots[0], "sub", lambda i: i ^ 1),
        swap(slots[1], "sub", lambda i: (((i - 1) % subs ^ 1) + 1) % subs),
        swap(slots[2], "seg", lambda i: i ^ 1),
        lax.ppermute(slots[3], "seg", inner),
    ]


def pair_sum(x):
    return x + swap(x, "seg", lambda i: i ^ 1)


def ring_swaps(x, axis, stride):
    return [swap(x, axis, lambda i, k=k: i ^ (k * stride)) for k in (1, 2, 3)]


def beside(work, *others):
    return lax.optimization_barrier((work, *others))


def add_all(x, parts):
    return (x + parts[0]) + (parts[1] + parts[2])


def body(nodal_loads, schur_matrix, face_rows, face_len, relax_step, coarse_basis, primal_index, coarse_inverse):
    loads, matrix, rows, basis = nodal_loads[0, 0], schur_matrix[0, 0], face_rows[0], coarse_basis[0, 0]
    block, width = loads.shape
    face_width = width // 4
    coarse_count = coarse_inverse.shape[0]

    shape = lambda *size: jax.ShapeDtypeStruct(size, F32)
    full, small, coarse_block = shape(block, width), shape(block, block), shape(block, coarse_count)
    terms = pltpu.VMEM((3 * block, width), BF16)
    hold = pltpu.VMEM((block, width), F32)
    faces = [shape(block, face_width)] * 4
    move = 2 * 3 * block * width * width
    turn = 2 * 2 * block * width * width
    light = 2 * 9 * block * block * width

    wide = [shape(block + 8, face_width)] * 4
    ints = lambda *size: jax.ShapeDtypeStruct(size, jnp.int32)
    table, *slots = on_core(
        first_gather, (face_len, primal_index, loads, basis, rows), (0, 1), [ints(INDEX + 32), *wide],
        [pltpu.VMEM((3 * (block + 16), width), BF16), pltpu.VMEM((block + 16, width), F32)], move, scalar_outs=(0,),
    )
    got = exchange(slots)
    weight, inverse, matrix = on_core(
        prepare, (table, rows, matrix), (0,), [shape(1, width), ints(1, width), jax.ShapeDtypeStruct((width, width), BF16)],
        [pltpu.VMEM((16, width), BF16), pltpu.SemaphoreType.DMA], move, far=(2,), limit=30 * MIB,
    )
    weight, *got = beside(weight, *got)
    residual, weighted, reach, coarse = on_core(
        first_scatter, (table, loads, basis, weight, inverse, *got), (0,),
        [full, full, jax.ShapeDtypeStruct((64, width), BF16), coarse_block],
        [pltpu.VMEM((3 * (block + 16), width), BF16)], move,
    )
    half_terms = pltpu.VMEM((2 * block, width), BF16)

    def one_sweep(*old):
        return on_core(
            functools.partial(first_sweep, not old), (relax_step, weighted, matrix, *old), (0,), [full], [half_terms], turn,
        )[0]

    coarse = pair_sum(coarse)
    for axis, stride in (("seg", 2), ("sub", 1), ("sub", 4)):
        parts = ring_swaps(coarse, axis, stride)
        solve = one_sweep() if axis == "seg" else one_sweep(solve)
        solve, *parts = beside(solve, *parts)
        coarse = add_all(coarse, parts)
    own, coarse_solution, *slots = on_core(
        first_correct, (table, solve, coarse, coarse_inverse, basis, weight, rows), (0,),
        [full, coarse_block, *faces], [terms, hold], move,
    )
    three = jax.ShapeDtypeStruct((3 * block, width), BF16)
    pair_terms = pltpu.VMEM((3 * block, width // 2), BF16)

    def add_pair(swaps, start, got):
        args = (table, start, inverse, *got)
        return on_core(functools.partial(add_faces, swaps), args, (0,), [full], [pair_terms], move // 2)[0]

    step = back = precond = direction = image = answer = curvature = rho = coarse_image = None
    for iteration in range(ITERS):
        first, last = iteration == 0, iteration + 1 == ITERS
        got = exchange(slots)
        settled = [solve, weighted, coarse_solution, coarse]
        outs = [small, small]
        if iteration:
            settled += [precond, step] + ([back, direction, answer] if iteration > 1 else [])
            outs += [full, three, full]
        settled = on_core(
            functools.partial(settle, iteration == 1, first), settled, (), outs, [terms, terms], light,
        )
        own = add_pair((2, 3), own, got[2:])
        own, local_rho, *got = beside(own, settled[0], *got[:2])
        coarse_rho = settled[1]
        if iteration:
            direction, direction_terms, answer = settled[2:]
        precond, partial, sums = on_core(
            functools.partial(apply_matrix, first),
            (table, own, local_rho, matrix, reach, inverse, *got, *(() if first else (direction_terms,))), (0,),
            [full, full, shape(block, PLACE + coarse_count)], [terms, terms], turn + move,
        )
        part = swap(sums, "seg", lambda i: i ^ 1)
        slots = on_core(gather_image, (table, partial, rows), (0,), faces, [terms, hold], move)
        part, *slots = beside(part, *slots)
        sums = sums + part
        parts = ring_swaps(sums, "seg", 2)
        got = exchange(slots)
        sums = add_all(sums, parts)
        image_part = add_pair((2, 3), partial, got[2:])
        image_part, sums, *got = beside(image_part, sums, *got[:2])
        parts = ring_swaps(sums, "sub", 1)
        image_part = add_pair((0, 1), image_part, got)
        image_part, *parts = beside(image_part, *parts)
        sums = add_all(sums, parts)
        parts = ring_swaps(sums, "sub", 4)
        args = [coarse_rho, image_part, residual]
        if not first:
            rho_inverse, = on_core(invert, (rho,), (), [small], [], light)
            rho_inverse, *parts = beside(rho_inverse, *parts)
            args += [image, curvature, rho_inverse]
        args = [add_all(sums, parts), *args]
        if last:
            answer, residual = on_core(
                functools.partial(advance, first, last), (*args, precond, direction, answer), (), [full, full], [], light,
            )
            break
        if not first:
            args += [coarse_image]
        at = len(args)
        args += [table, relax_step, matrix, weight, basis, rows, coarse, coarse_inverse]
        outs = [full, full, small, small, small] + ([] if first else [small])
        outs += [coarse_block, coarse_block, coarse_block, full, full, full, *faces]
        residual, image, curvature, rho, step, *rest = on_core(
            functools.partial(advance, first, last), args, (at, at + 1), outs, [terms, hold], 3 * turn + move,
        )
        if not first:
            back = rest.pop(0)
        coarse_image, coarse, coarse_solution, solve, weighted, own, *slots = rest
    return (answer[None, None], residual[None, None])


def solution(mesh):
    placed = (
        P("seg", "sub", None, None),
        P("seg", "sub", None, None),
        P("seg", "sub", None),
        P(),
        P("seg", "sub"),
        P("seg", "sub", None, None),
        P(),
        P(),
    )
    return jax.shard_map(
        body,
        mesh=mesh,
        in_specs=placed,
        out_specs=(P("seg", "sub", None, None), P("seg", "sub", None, None)),
        check_vma=False,
    )
```

```python
import functools

import jax
import jax.numpy as jnp
from jax import lax
from jax.experimental import pallas as pl
from jax.experimental.pallas import tpu as pltpu
from jax.sharding import PartitionSpec as P

DEG = 3
ITERS = 3
HIGH = lax.Precision.HIGHEST
F32 = jnp.float32
BF16 = jnp.bfloat16
MIB = 1 << 20

PLACE = 128
FACE = 4
INDEX = 8
MEMBERS = (0, 1, 2, 3) + tuple(range(16, 32))


def dot(a, b):
    return jnp.dot(a, b, precision=HIGH, preferred_element_type=F32)


def symmetric(matrix):
    return 0.5 * (matrix + matrix.T)


def two_terms(x):
    hi = x.astype(BF16)
    return hi, (x - hi.astype(F32)).astype(BF16)


def three_terms(x):
    hi = x.astype(BF16)
    rest = x - hi.astype(F32)
    mid = rest.astype(BF16)
    return hi, mid, (rest - mid.astype(F32)).astype(BF16)


def put_terms(ref, first, columns, terms):
    rows = terms[0].shape[0]
    for at, term in enumerate(terms):
        ref[first + at * rows : first + (at + 1) * rows, columns] = term


def fold(y, parts):
    rows = y.shape[0] // parts
    total = y[:rows]
    for at in range(1, parts):
        total = total + y[at * rows : (at + 1) * rows]
    return total


def gram(left, right, left_parts, right_parts):
    y = lax.dot_general(left, right, (((1,), (1,)), ((), ())), preferred_element_type=F32)
    y = fold(y, left_parts)
    columns = y.shape[1] // right_parts
    total = y[:, :columns]
    for at in range(1, right_parts):
        total = total + y[:, at * columns : (at + 1) * columns]
    return total


def stacked(matrix):
    return jnp.concatenate([jnp.concatenate([term] * 3, axis=1) for term in three_terms(matrix)], axis=0)


def mix(stack, x):
    terms = jnp.concatenate(three_terms(x), axis=0)
    return fold(jnp.dot(stack, terms, preferred_element_type=F32), 3)


def cut(width, parts):
    return width // parts if width % parts == 0 and (width // parts) % 128 == 0 else width // 4


def over_columns(width, parts, one):
    tile = cut(width, parts)

    def step(t, carry):
        start = pl.multiple_of(t * tile, tile)
        one(pl.ds(start, tile), start, tile)
        return carry

    lax.fori_loop(0, width // tile, step, 0)


def spd_solve(a, b):
    n = a.shape[0]
    both = jnp.concatenate([a, b], axis=1)
    row = lax.broadcasted_iota(jnp.int32, (n, 1), 0)
    for k in range(n):
        pivot = both[k : k + 1, :] / both[k : k + 1, k : k + 1]
        both = jnp.where(row == k, pivot, both - both[:, k : k + 1] * pivot)
    return both[:, n:]


def one_hot(index, chunk, within):
    low = jnp.where(index // 256 == chunk, (index % 256).astype(F32), -1.0).astype(BF16)
    return jnp.where(within == low, jnp.ones((), BF16), jnp.zeros((), BF16))


def within_chunk(columns):
    return lax.broadcasted_iota(jnp.int32, (256, columns), 0).astype(F32).astype(BF16)


def permute(terms_ref, index_ref, chunks, emit):
    within = within_chunk(cut(index_ref.shape[1], 4))

    def one(columns, start, tile):
        index = index_ref[0:1, columns]
        y = None
        for at, chunk in enumerate(chunks):
            hot = one_hot(index, chunk, within)
            part = jnp.dot(terms_ref[:, at * 256 : (at + 1) * 256], hot, preferred_element_type=F32)
            y = part if y is None else y + part
        emit(columns, fold(y, 3))

    over_columns(index_ref.shape[1], 4, one)


def face_columns(table_ref, swap, face_width):
    return pl.ds(pl.multiple_of(table_ref[FACE + swap] * face_width, face_width), face_width)


def gather_slots(x, terms_ref, rows_ref, table_ref, hold_ref, out_refs):
    put_terms(terms_ref, 0, slice(None), three_terms(x))

    def emit(columns, y):
        hold_ref[:, columns] = y

    permute(terms_ref, rows_ref, range(rows_ref.shape[1] // 256), emit)
    face_width = rows_ref.shape[1] // 4
    at = lax.broadcasted_iota(jnp.int32, (1, face_width), 1)
    for swap, out in enumerate(out_refs):
        part = hold_ref[0 : out.shape[0], face_columns(table_ref, swap, face_width)]
        out[...] = part * (at < table_ref[swap]).astype(F32)


def face_chunks(swaps, table_ref, face_width):
    each = face_width // 256
    return [table_ref[FACE + swap] * each + part for swap in swaps for part in range(each)]


def scatter_faces(in_refs, swaps, terms_ref, inverse_ref, table_ref, emit):
    face_width = inverse_ref.shape[1] // 4
    for at, ref in enumerate(in_refs):
        put_terms(terms_ref, 0, slice(at * face_width, (at + 1) * face_width), three_terms(ref[...]))
    permute(terms_ref, inverse_ref, face_chunks(swaps, table_ref, face_width), emit)


def product(terms_ref, matrix_ref, emit):
    def one(columns, start, tile):
        emit(columns, fold(jnp.dot(terms_ref[...], matrix_ref[:, columns], preferred_element_type=F32), 2))

    over_columns(matrix_ref.shape[1], 3, one)


def sweep(weighted_ref, solve_ref, terms_ref, relax, matrix_ref):
    put_terms(terms_ref, 0, slice(None), two_terms(solve_ref[...]))

    def emit(columns, y):
        solve_ref[:, columns] = relax * weighted_ref[:, columns] + solve_ref[:, columns] - relax * y

    product(terms_ref, matrix_ref, emit)


def place(columns, table_ref, members, width):
    at = lax.broadcasted_iota(jnp.int32, (1, width), 1)
    total = jnp.zeros((columns.shape[0], width), F32)
    for member in members:
        total = total + columns[:, member : member + 1] * (at == table_ref[INDEX + member]).astype(F32)
    return total


def correct(solve_ref, coarse_solution, table_ref, basis_ref, weight_ref):
    at = lax.broadcasted_iota(jnp.int32, (1, coarse_solution.shape[1]), 1)
    solve = solve_ref[...]
    for face in range(4):
        mine = (at == table_ref[INDEX + face]).astype(F32)
        picked = jnp.sum(coarse_solution * mine, axis=1, keepdims=True)
        solve = solve + picked * basis_ref[face : face + 1, :]
    return solve * weight_ref[...]


def fill_table(table_ref, face_len_ref, primal_ref):
    s, j = lax.axis_index("seg"), lax.axis_index("sub")
    segs, subs = face_len_ref.shape[:2]
    left, right = lax.rem(j + subs - 1, subs), lax.rem(j + 1, subs)
    down, up = jnp.maximum(s - 1, 0), jnp.minimum(s + 1, segs - 1)
    sub_odd, seg_odd = lax.rem(j, 2), lax.rem(s, 2)
    lengths = (
        face_len_ref[s, left, 0],
        face_len_ref[s, j, 0],
        jnp.where(s > 0, face_len_ref[down, j, 1], 0),
        jnp.where(s < segs - 1, face_len_ref[s, j, 1], 0),
    )
    table_ref[0] = jnp.where(sub_odd == 0, lengths[1], lengths[0])
    table_ref[1] = jnp.where(sub_odd == 0, lengths[0], lengths[1])
    table_ref[2] = jnp.where(seg_odd == 0, lengths[3], lengths[2])
    table_ref[3] = jnp.where(seg_odd == 0, lengths[2], lengths[3])
    table_ref[FACE] = 1 - sub_odd
    table_ref[FACE + 1] = sub_odd
    table_ref[FACE + 2] = 3 - seg_odd
    table_ref[FACE + 3] = 2 + seg_odd
    for at, (row, column) in enumerate(((s, j), (s, left), (s, right), (down, j), (up, j))):
        first = INDEX if at == 0 else INDEX + 12 + 4 * at
        for face in range(4):
            table_ref[first + face] = primal_ref[row, column, face]


def first_gather(
    face_len_ref, primal_ref, loads_ref, basis_ref, rows_ref, table_ref, o0, o1, o2, o3, terms_ref, hold_ref
):
    fill_table(table_ref, face_len_ref, primal_ref)
    spare = jnp.zeros((12, loads_ref.shape[1]), F32)
    x = jnp.concatenate([loads_ref[...], 0.5 * basis_ref[...], spare], axis=0)
    gather_slots(x, terms_ref, rows_ref, table_ref, hold_ref, (o0, o1, o2, o3))


def prepare(table_ref, rows_ref, matrix_at, weight_ref, inverse_ref, matrix_ref, terms_ref, sem):
    copy = pltpu.make_async_copy(matrix_at, matrix_ref, sem)
    copy.start()
    width = rows_ref.shape[1]
    face_width = width // 4
    row = lax.broadcasted_iota(jnp.int32, (16, face_width), 0)
    column = lax.broadcasted_iota(jnp.int32, (16, face_width), 1)
    for swap in range(4):
        slot = column + table_ref[FACE + swap] * face_width
        weight = 1.0 - 0.5 * (column < table_ref[swap]).astype(F32)
        extra = jnp.where(
            row == 0,
            weight,
            jnp.where(row == 1, (slot // 256).astype(F32), jnp.where(row == 2, (slot % 256).astype(F32), 0.0)),
        )
        terms_ref[:, face_columns(table_ref, swap, face_width)] = extra.astype(BF16)
    within = within_chunk(width)

    def one(chunk, carry):
        columns = pl.ds(pl.multiple_of(chunk * 256, 256), 256)
        hot = one_hot(rows_ref[...], chunk, within)
        y = lax.dot_general(terms_ref[...], hot, (((1,), (1,)), ((), ())), preferred_element_type=F32)
        weight_ref[:, columns] = y[0:1]
        inverse_ref[:, columns] = (y[1:2] * 256.0 + y[2:3]).astype(jnp.int32)
        return carry

    lax.fori_loop(0, width // 256, one, 0)
    copy.wait()


def first_scatter(
    table_ref, loads_ref, basis_ref, weight_ref, inverse_ref, i0, i1, i2, i3,
    residual_ref, weighted_ref, reach_ref, coarse_ref, terms_ref,
):
    block, width = loads_ref.shape
    face_width = width // 4
    row = lax.broadcasted_iota(jnp.int32, (16, face_width), 0)
    for swap, ref in enumerate((i0, i1, i2, i3)):
        face = table_ref[FACE + swap]
        got = ref[block : block + 4, :]
        spread = jnp.where(row // 4 == face, jnp.concatenate([got] * 4, axis=0), 0.0)
        both = jnp.concatenate([ref[0:block, :], spread], axis=0)
        put_terms(terms_ref, 0, slice(swap * face_width, (swap + 1) * face_width), three_terms(both))

    def gain(columns, y):
        residual = loads_ref[:, columns] + y[:block]
        weight = weight_ref[:, columns]
        residual_ref[:, columns] = residual
        weighted_ref[:, columns] = residual * weight
        blank = jnp.zeros((12, y.shape[1]), F32)
        reach = jnp.concatenate([weight * basis_ref[:, columns], blank, y[block:]], axis=0)
        put_terms(reach_ref, 0, columns, two_terms(reach))

    permute(terms_ref, inverse_ref, face_chunks(range(4), table_ref, face_width), gain)
    coarse = lax.dot_general(
        weighted_ref[...], basis_ref[...], (((1,), (1,)), ((), ())), precision=HIGH, preferred_element_type=F32
    )
    coarse_ref[...] = place(coarse, table_ref, range(4), coarse_ref.shape[1])


def first_sweep(begin, *refs):
    if begin:
        relax_ref, weighted_ref, matrix_ref, solve_ref, terms_ref = refs
        solve_ref[...] = relax_ref[0, 0] * weighted_ref[...]
    else:
        relax_ref, weighted_ref, matrix_ref, old_ref, solve_ref, terms_ref = refs
        solve_ref[...] = old_ref[...]
    sweep(weighted_ref, solve_ref, terms_ref, relax_ref[0, 0], matrix_ref)


def first_own(table_ref, solve_ref, weight_ref, rows_ref, own_ref, o0, o1, o2, o3, terms_ref, hold_ref):
    own_ref[...] = solve_ref[...] * weight_ref[...]
    gather_slots(own_ref[...], terms_ref, rows_ref, table_ref, hold_ref, (o0, o1, o2, o3))


def settle(first, start, *refs):
    refs = list(refs)
    solve_ref, weighted_ref, coarse_solution_ref, coarse_ref = refs[:4]
    rest = refs[4:]
    if start:
        coarse_inverse_ref = coarse_solution_ref
        rho_ref, coarse_rho_ref, coarse_solution_ref, left_ref, right_ref = rest
        coarse_solution_ref[...] = dot(coarse_ref[...], coarse_inverse_ref[...])
    else:
        whole_rho_ref, precond_ref, step_ref = rest[:3]
        rest = rest[3:]
        if not first:
            back_ref, old_direction_ref, old_solution_ref = rest[:3]
            rest = rest[3:]
        rho_ref, coarse_rho_ref, rho_inverse_ref, direction_ref, direction_terms_ref, solution_ref, left_ref, right_ref = rest
    put_terms(left_ref, 0, slice(None), three_terms(solve_ref[...]))
    put_terms(right_ref, 0, slice(None), three_terms(weighted_ref[...]))
    rho_ref[...] = gram(left_ref[...], right_ref[...], 3, 3)
    coarse_rho_ref[...] = lax.dot_general(
        coarse_solution_ref[...], coarse_ref[...], (((1,), (1,)), ((), ())), precision=HIGH, preferred_element_type=F32
    )
    if start:
        return
    n = whole_rho_ref.shape[0]
    row = lax.broadcasted_iota(jnp.int32, (n, n), 0)
    one = (row == lax.broadcasted_iota(jnp.int32, (n, n), 1)).astype(F32)
    rho_inverse_ref[...] = spd_solve(whole_rho_ref[...], one)
    step = stacked(step_ref[...])
    back = None if first else stacked(back_ref[...])

    def turn(columns, start_at, tile):
        direction = precond_ref[:, columns]
        if not first:
            direction = direction + mix(back, old_direction_ref[:, columns])
        direction_ref[:, columns] = direction
        put_terms(direction_terms_ref, 0, columns, three_terms(direction))
        moved = mix(step, direction)
        solution_ref[:, columns] = moved if first else old_solution_ref[:, columns] + moved

    over_columns(solve_ref.shape[1], 4, turn)


def apply_matrix(first, *refs):
    refs = list(refs)
    table_ref, own_ref, rho_ref, matrix_ref, reach_ref, inverse_ref = refs[:6]
    ins, rest = refs[6:10], refs[10:]
    if first:
        coarse_solution_ref = rest.pop(0)
    else:
        direction_terms_ref = rest.pop(0)
    precond_ref, partial_ref, sums_ref, terms_ref, more_ref = rest
    block = own_ref.shape[0]

    if first:
        width = coarse_solution_ref.shape[1]
        row = lax.broadcasted_iota(jnp.int32, (32, width), 0)
        at = lax.broadcasted_iota(jnp.int32, (32, width), 1)
        pick = jnp.zeros((32, width), F32)
        for member in MEMBERS:
            pick = jnp.where((row == member) & (at == table_ref[INDEX + member]), 1.0, pick)
        picked = lax.dot_general(
            coarse_solution_ref[...], pick, (((1,), (1,)), ((), ())), precision=HIGH, preferred_element_type=F32
        )
        picks = jnp.concatenate([jnp.concatenate([term] * 2, axis=1) for term in three_terms(picked)], axis=0)

    def gain(columns, y):
        precond = own_ref[:, columns] + y
        if first:
            precond = precond + fold(jnp.dot(picks, reach_ref[:, columns], preferred_element_type=F32), 3)
        precond_ref[:, columns] = precond

    scatter_faces(ins, range(4), terms_ref, inverse_ref, table_ref, gain)
    put_terms(terms_ref, 0, slice(None), three_terms(precond_ref[...]))
    put_terms(more_ref, 0, slice(None), two_terms(precond_ref[...]))

    def emit(columns, y):
        partial_ref[:, columns] = y

    product(more_ref.at[0 : 2 * block], matrix_ref, emit)
    put_terms(more_ref, 0, slice(None), three_terms(partial_ref[...]))
    partial = more_ref[...]
    sums_ref[:, 0:PLACE] = jnp.zeros((block, PLACE), F32)
    sums_ref[:, 0:block] = rho_ref[...]
    sums_ref[:, block : 2 * block] = gram(partial, terms_ref[...], 3, 3)
    if not first:
        sums_ref[:, 2 * block : 3 * block] = gram(partial, direction_terms_ref[...], 3, 3)
    coarse = gram(partial, reach_ref[...], 3, 2)
    sums_ref[:, PLACE:] = place(coarse, table_ref, MEMBERS, sums_ref.shape[1] - PLACE)


def gather_image(table_ref, partial_ref, rows_ref, o0, o1, o2, o3, terms_ref, hold_ref):
    gather_slots(partial_ref[...], terms_ref, rows_ref, table_ref, hold_ref, (o0, o1, o2, o3))


def scatter_image(table_ref, partial_ref, inverse_ref, i0, i1, i2, i3, image_ref, terms_ref):
    def gain(columns, y):
        image_ref[:, columns] = partial_ref[:, columns] + y

    scatter_faces((i0, i1, i2, i3), range(4), terms_ref, inverse_ref, table_ref, gain)


def advance(first, last, *refs):
    refs = list(refs)
    sums_ref, coarse_rho_ref, image_part_ref, residual_ref = refs[:4]
    rest = refs[4:]
    if not first:
        old_image_ref, old_curvature_ref, old_rho_inverse_ref = rest[:3]
        rest = rest[3:]
    if last:
        precond_ref, old_direction_ref, old_solution_ref, new_solution_ref, new_residual_ref = rest
    else:
        if not first:
            old_coarse_image_ref = rest.pop(0)
        table_ref, relax_ref, matrix_ref, weight_ref, basis_ref, rows_ref, coarse_ref, coarse_inverse_ref = rest[:8]
        rest = rest[8:]
        new_residual_ref, image_ref, curvature_ref, rho_out_ref, step_ref = rest[:5]
        rest = rest[5:]
        if not first:
            back_ref = rest.pop(0)
        coarse_image_ref, new_coarse_ref, coarse_solution_ref, solve_ref, weighted_ref, own_ref = rest[:6]
        o0, o1, o2, o3, terms_ref, hold_ref = rest[6:]
    block, width = residual_ref.shape
    rho = symmetric(sums_ref[:, 0:block] + coarse_rho_ref[...])
    curvature = symmetric(sums_ref[:, block : 2 * block])
    if not first:
        beta = dot(old_rho_inverse_ref[...], rho)
        back = beta.T
        cross = dot(sums_ref[:, 2 * block : 3 * block], beta)
        curvature = curvature + (cross + cross.T) + symmetric(dot(back, dot(old_curvature_ref[...], beta)))
        back_stack = stacked(back)
    step = spd_solve(curvature, rho).T
    step_stack = stacked(step)

    def one(columns, start, tile):
        image = image_part_ref[:, columns]
        if not first:
            image = image + mix(back_stack, old_image_ref[:, columns])
        residual = residual_ref[:, columns] - mix(step_stack, image)
        new_residual_ref[:, columns] = residual
        if last:
            direction = precond_ref[:, columns] + mix(back_stack, old_direction_ref[:, columns])
            new_solution_ref[:, columns] = old_solution_ref[:, columns] + mix(step_stack, direction)
        else:
            image_ref[:, columns] = image
            weighted = residual * weight_ref[:, columns]
            weighted_ref[:, columns] = weighted
            solve_ref[:, columns] = relax_ref[0, 0] * weighted

    over_columns(width, 4, one)
    if last:
        return
    step_ref[...] = step
    curvature_ref[...] = curvature
    rho_out_ref[...] = rho
    coarse_image = sums_ref[:, PLACE:]
    if not first:
        back_ref[...] = back
        coarse_image = coarse_image + dot(back, old_coarse_image_ref[...])
    coarse_image_ref[...] = coarse_image
    coarse = coarse_ref[...] - dot(step, coarse_image)
    new_coarse_ref[...] = coarse
    coarse_solution = dot(coarse, coarse_inverse_ref[...])
    coarse_solution_ref[...] = coarse_solution

    def again(t, carry):
        sweep(weighted_ref, solve_ref, terms_ref.at[0 : 2 * block], relax_ref[0, 0], matrix_ref)
        return carry

    lax.fori_loop(0, DEG, again, 0)
    own_ref[...] = correct(solve_ref, coarse_solution, table_ref, basis_ref, weight_ref)
    gather_slots(own_ref[...], terms_ref, rows_ref, table_ref, hold_ref, (o0, o1, o2, o3))


def on_core(kernel, args, scalars, outs, scratch, flops, far=(), scalar_outs=(), limit=12 * MIB):
    def spec(at, scalar, far):
        return pl.BlockSpec(memory_space=pltpu.SMEM if at in scalar else pltpu.HBM if at in far else pltpu.VMEM)

    size = sum(x.size * x.dtype.itemsize for x in args) + sum(4 * o.size for o in outs)
    return pl.pallas_call(
        kernel,
        out_shape=outs,
        in_specs=[spec(at, scalars, far) for at in range(len(args))],
        out_specs=[spec(at, scalar_outs, ()) for at in range(len(outs))],
        scratch_shapes=scratch,
        compiler_params=pltpu.CompilerParams(vmem_limit_bytes=limit),
        cost_estimate=pl.CostEstimate(flops=flops, bytes_accessed=size, transcendentals=0),
    )(*args)


def swap(x, axis, partner):
    return lax.ppermute(x, axis, [(i, partner(i)) for i in range(lax.axis_size(axis))])


def exchange(slots):
    subs, segs = lax.axis_size("sub"), lax.axis_size("seg")
    inner = [(i, ((i - 1) ^ 1) + 1) for i in range(1, segs - 1)]
    return [
        swap(slots[0], "sub", lambda i: i ^ 1),
        swap(slots[1], "sub", lambda i: (((i - 1) % subs ^ 1) + 1) % subs),
        swap(slots[2], "seg", lambda i: i ^ 1),
        lax.ppermute(slots[3], "seg", inner),
    ]


def ring_swaps(x, axis, stride):
    return [swap(x, axis, lambda i, k=k: i ^ (k * stride)) for k in (1, 2, 3)]


def beside(work, *others):
    return lax.optimization_barrier((work, *others))


def add_all(x, parts):
    return (x + parts[0]) + (parts[1] + parts[2])


def body(nodal_loads, schur_matrix, face_rows, face_len, relax_step, coarse_basis, primal_index, coarse_inverse):
    loads, matrix, rows, basis = nodal_loads[0, 0], schur_matrix[0, 0], face_rows[0], coarse_basis[0, 0]
    block, width = loads.shape
    face_width = width // 4
    coarse_count = coarse_inverse.shape[0]

    shape = lambda *size: jax.ShapeDtypeStruct(size, F32)
    full, small, coarse_block = shape(block, width), shape(block, block), shape(block, coarse_count)
    terms = pltpu.VMEM((3 * block, width), BF16)
    hold = pltpu.VMEM((block, width), F32)
    faces = [shape(block, face_width)] * 4
    move = 2 * 3 * block * width * width
    turn = 2 * 2 * block * width * width
    light = 2 * 9 * block * block * width

    wide = [shape(block + 8, face_width)] * 4
    ints = lambda *size: jax.ShapeDtypeStruct(size, jnp.int32)
    table, *slots = on_core(
        first_gather, (face_len, primal_index, loads, basis, rows), (0, 1), [ints(INDEX + 32), *wide],
        [pltpu.VMEM((3 * (block + 16), width), BF16), pltpu.VMEM((block + 16, width), F32)], move, scalar_outs=(0,),
    )
    got = exchange(slots)
    weight, inverse, matrix = on_core(
        prepare, (table, rows, matrix), (0,), [shape(1, width), ints(1, width), jax.ShapeDtypeStruct((width, width), BF16)],
        [pltpu.VMEM((16, width), BF16), pltpu.SemaphoreType.DMA], move, far=(2,), limit=30 * MIB,
    )
    weight, *got = beside(weight, *got)
    residual, weighted, reach, coarse = on_core(
        first_scatter, (table, loads, basis, weight, inverse, *got), (0,),
        [full, full, jax.ShapeDtypeStruct((64, width), BF16), coarse_block],
        [pltpu.VMEM((3 * (block + 16), width), BF16)], move,
    )
    half_terms = pltpu.VMEM((2 * block, width), BF16)

    def one_sweep(*old):
        return on_core(
            functools.partial(first_sweep, not old), (relax_step, weighted, matrix, *old), (0,), [full], [half_terms], turn,
        )[0]

    part = swap(coarse, "seg", lambda i: i ^ 1)
    solve, part = beside(one_sweep(), part)
    coarse = coarse + part
    parts = ring_swaps(coarse, "seg", 2)
    solve, *parts = beside(one_sweep(solve), *parts)
    coarse = add_all(coarse, parts)
    parts = ring_swaps(coarse, "sub", 1)
    solve = one_sweep(solve)
    own, *slots = on_core(first_own, (table, solve, weight, rows), (0,), [full, *faces], [terms, hold], move)
    own, *parts = beside(own, *parts)
    coarse = add_all(coarse, parts)
    three = jax.ShapeDtypeStruct((3 * block, width), BF16)
    step = back = precond = coarse_solution = direction = image = answer = curvature = rho = coarse_image = None
    for iteration in range(ITERS):
        first, last = iteration == 0, iteration + 1 == ITERS
        if first:
            parts = ring_swaps(coarse, "sub", 4)
        got = exchange(slots)
        if first:
            coarse = add_all(coarse, parts)
        settled = [solve, weighted, coarse_inverse if first else coarse_solution, coarse]
        outs = [small, small] + ([coarse_block] if first else [])
        if iteration:
            settled += [rho, precond, step] + ([back, direction, answer] if iteration > 1 else [])
            outs += [small, full, three, full]
        settled = on_core(
            functools.partial(settle, iteration == 1, first), settled, (), outs, [terms, terms], light,
        )
        local_rho, *got = beside(settled[0], *got)
        coarse_rho = settled[1]
        if first:
            coarse_solution = settled[2]
        else:
            rho_inverse, direction, direction_terms, answer = settled[2:]
        precond, partial, sums = on_core(
            functools.partial(apply_matrix, first),
            (table, own, local_rho, matrix, reach, inverse, *got, coarse_solution if first else direction_terms), (0,),
            [full, full, shape(block, PLACE + coarse_count)], [terms, terms], turn + move,
        )
        part = swap(sums, "seg", lambda i: i ^ 1)
        slots = on_core(gather_image, (table, partial, rows), (0,), faces, [terms, hold], move)
        part, *slots = beside(part, *slots)
        sums = sums + part
        parts = ring_swaps(sums, "seg", 2)
        got = exchange(slots)
        sums = add_all(sums, parts)
        sums, *got = beside(sums, *got)
        parts = ring_swaps(sums, "sub", 1)
        image_part, = on_core(scatter_image, (table, partial, inverse, *got), (0,), [full], [terms], move)
        image_part, *parts = beside(image_part, *parts)
        sums = add_all(sums, parts)
        parts = ring_swaps(sums, "sub", 4)
        args = [coarse_rho, image_part, residual]
        if not first:
            args += [image, curvature, rho_inverse]
        args = [add_all(sums, parts), *args]
        if last:
            answer, residual = on_core(
                functools.partial(advance, first, last), (*args, precond, direction, answer), (), [full, full], [], light,
            )
            break
        if not first:
            args += [coarse_image]
        at = len(args)
        args += [table, relax_step, matrix, weight, basis, rows, coarse, coarse_inverse]
        outs = [full, full, small, small, small] + ([] if first else [small])
        outs += [coarse_block, coarse_block, coarse_block, full, full, full, *faces]
        residual, image, curvature, rho, step, *rest = on_core(
            functools.partial(advance, first, last), args, (at, at + 1), outs, [terms, hold], 3 * turn + move,
        )
        if not first:
            back = rest.pop(0)
        coarse_image, coarse, coarse_solution, solve, weighted, own, *slots = rest
    return (answer[None, None], residual[None, None])


def solution(mesh):
    placed = (
        P("seg", "sub", None, None),
        P("seg", "sub", None, None),
        P("seg", "sub", None),
        P(),
        P("seg", "sub"),
        P("seg", "sub", None, None),
        P(),
        P(),
    )
    return jax.shard_map(
        body,
        mesh=mesh,
        in_specs=placed,
        out_specs=(P("seg", "sub", None, None), P("seg", "sub", None, None)),
        check_vma=False,
    )
```

```python
import functools

import jax
import jax.numpy as jnp
from jax import lax
from jax.experimental import pallas as pl
from jax.experimental.pallas import tpu as pltpu
from jax.sharding import PartitionSpec as P

DEG = 3
ITERS = 3
HIGH = lax.Precision.HIGHEST
F32 = jnp.float32
BF16 = jnp.bfloat16
MIB = 1 << 20

PLACE = 128
FACE = 4
INDEX = 8
MEMBERS = (0, 1, 2, 3) + tuple(range(16, 32))


def dot(a, b):
    return jnp.dot(a, b, precision=HIGH, preferred_element_type=F32)


def symmetric(matrix):
    return 0.5 * (matrix + matrix.T)


def two_terms(x):
    hi = x.astype(BF16)
    return hi, (x - hi.astype(F32)).astype(BF16)


def three_terms(x):
    hi = x.astype(BF16)
    rest = x - hi.astype(F32)
    mid = rest.astype(BF16)
    return hi, mid, (rest - mid.astype(F32)).astype(BF16)


def put_terms(ref, first, columns, terms):
    rows = terms[0].shape[0]
    for at, term in enumerate(terms):
        ref[first + at * rows : first + (at + 1) * rows, columns] = term


def fold(y, parts):
    rows = y.shape[0] // parts
    total = y[:rows]
    for at in range(1, parts):
        total = total + y[at * rows : (at + 1) * rows]
    return total


def gram(left, right, left_parts, right_parts):
    y = lax.dot_general(left, right, (((1,), (1,)), ((), ())), preferred_element_type=F32)
    y = fold(y, left_parts)
    columns = y.shape[1] // right_parts
    total = y[:, :columns]
    for at in range(1, right_parts):
        total = total + y[:, at * columns : (at + 1) * columns]
    return total


def stacked(matrix):
    return jnp.concatenate([jnp.concatenate([term] * 3, axis=1) for term in three_terms(matrix)], axis=0)


def mix(stack, x):
    terms = jnp.concatenate(three_terms(x), axis=0)
    return fold(jnp.dot(stack, terms, preferred_element_type=F32), 3)


def cut(width, parts):
    return width // parts if width % parts == 0 and (width // parts) % 128 == 0 else width // 4


def over_columns(width, parts, one):
    tile = cut(width, parts)

    def step(t, carry):
        start = pl.multiple_of(t * tile, tile)
        one(pl.ds(start, tile), start, tile)
        return carry

    lax.fori_loop(0, width // tile, step, 0)


def spd_solve(a, b):
    n, block = a.shape[0], 8
    both = jnp.concatenate([a, b], axis=1)
    row = lax.broadcasted_iota(jnp.int32, (n, 1), 0)
    for k in range(0, n, block):
        columns = [jnp.broadcast_to(both[:, k + j : k + j + 1], both.shape) for j in range(block)]
        rows = [both[k + i : k + i + 1, :] for i in range(block)]
        small = [[columns[j][k + i : k + i + 1, :] for j in range(block)] for i in range(block)]
        for p in range(block):
            over = 1.0 / small[p][p]
            rows[p] = rows[p] * over
            for j in range(p + 1, block):
                small[p][j] = small[p][j] * over
            for i in range(block):
                if i != p:
                    rows[i] = rows[i] - small[i][p] * rows[p]
                    for j in range(p + 1, block):
                        small[i][j] = small[i][j] - small[i][p] * small[p][j]
        after = both
        for j in range(block):
            after = after - columns[j] * rows[j]
        for j in range(block):
            after = jnp.where(row == k + j, rows[j], after)
        both = after
    return both[:, n:]


def one_hot(index, chunk, within):
    low = jnp.where(index // 256 == chunk, (index % 256).astype(F32), -1.0).astype(BF16)
    return jnp.where(within == low, jnp.ones((), BF16), jnp.zeros((), BF16))


def within_chunk(columns):
    return lax.broadcasted_iota(jnp.int32, (256, columns), 0).astype(F32).astype(BF16)


def permute(terms_ref, index_ref, chunks, emit):
    within = within_chunk(cut(index_ref.shape[1], 4))

    def one(columns, start, tile):
        index = index_ref[0:1, columns]
        y = None
        for at, chunk in enumerate(chunks):
            hot = one_hot(index, chunk, within)
            part = jnp.dot(terms_ref[:, at * 256 : (at + 1) * 256], hot, preferred_element_type=F32)
            y = part if y is None else y + part
        emit(columns, fold(y, 3))

    over_columns(index_ref.shape[1], 4, one)


def face_columns(table_ref, swap, face_width):
    return pl.ds(pl.multiple_of(table_ref[FACE + swap] * face_width, face_width), face_width)


def gather_slots(x, terms_ref, rows_ref, table_ref, hold_ref, out_refs):
    put_terms(terms_ref, 0, slice(None), three_terms(x))

    def emit(columns, y):
        hold_ref[:, columns] = y

    permute(terms_ref, rows_ref, range(rows_ref.shape[1] // 256), emit)
    face_width = rows_ref.shape[1] // 4
    at = lax.broadcasted_iota(jnp.int32, (1, face_width), 1)
    for swap, out in enumerate(out_refs):
        part = hold_ref[0 : out.shape[0], face_columns(table_ref, swap, face_width)]
        out[...] = part * (at < table_ref[swap]).astype(F32)


def face_chunks(swaps, table_ref, face_width):
    each = face_width // 256
    return [table_ref[FACE + swap] * each + part for swap in swaps for part in range(each)]


def scatter_faces(in_refs, swaps, terms_ref, inverse_ref, table_ref, emit):
    face_width = inverse_ref.shape[1] // 4
    for at, ref in enumerate(in_refs):
        put_terms(terms_ref, 0, slice(at * face_width, (at + 1) * face_width), three_terms(ref[...]))
    permute(terms_ref, inverse_ref, face_chunks(swaps, table_ref, face_width), emit)


def product(terms_ref, matrix_ref, emit):
    def one(columns, start, tile):
        emit(columns, fold(jnp.dot(terms_ref[...], matrix_ref[:, columns], preferred_element_type=F32), 2))

    over_columns(matrix_ref.shape[1], 3, one)


def sweep(weighted_ref, solve_ref, terms_ref, relax, matrix_ref):
    put_terms(terms_ref, 0, slice(None), two_terms(solve_ref[...]))

    def emit(columns, y):
        solve_ref[:, columns] = relax * weighted_ref[:, columns] + solve_ref[:, columns] - relax * y

    product(terms_ref, matrix_ref, emit)


def place(columns, table_ref, members, width):
    at = lax.broadcasted_iota(jnp.int32, (1, width), 1)
    total = jnp.zeros((columns.shape[0], width), F32)
    for member in members:
        total = total + columns[:, member : member + 1] * (at == table_ref[INDEX + member]).astype(F32)
    return total


def correct(solve_ref, coarse_solution, table_ref, basis_ref, weight_ref):
    at = lax.broadcasted_iota(jnp.int32, (1, coarse_solution.shape[1]), 1)
    solve = solve_ref[...]
    for face in range(4):
        mine = (at == table_ref[INDEX + face]).astype(F32)
        picked = jnp.sum(coarse_solution * mine, axis=1, keepdims=True)
        solve = solve + picked * basis_ref[face : face + 1, :]
    return solve * weight_ref[...]


def fill_table(table_ref, face_len_ref, primal_ref):
    s, j = lax.axis_index("seg"), lax.axis_index("sub")
    segs, subs = face_len_ref.shape[:2]
    left, right = lax.rem(j + subs - 1, subs), lax.rem(j + 1, subs)
    down, up = jnp.maximum(s - 1, 0), jnp.minimum(s + 1, segs - 1)
    sub_odd, seg_odd = lax.rem(j, 2), lax.rem(s, 2)
    lengths = (
        face_len_ref[s, left, 0],
        face_len_ref[s, j, 0],
        jnp.where(s > 0, face_len_ref[down, j, 1], 0),
        jnp.where(s < segs - 1, face_len_ref[s, j, 1], 0),
    )
    table_ref[0] = jnp.where(sub_odd == 0, lengths[1], lengths[0])
    table_ref[1] = jnp.where(sub_odd == 0, lengths[0], lengths[1])
    table_ref[2] = jnp.where(seg_odd == 0, lengths[3], lengths[2])
    table_ref[3] = jnp.where(seg_odd == 0, lengths[2], lengths[3])
    table_ref[FACE] = 1 - sub_odd
    table_ref[FACE + 1] = sub_odd
    table_ref[FACE + 2] = 3 - seg_odd
    table_ref[FACE + 3] = 2 + seg_odd
    for at, (row, column) in enumerate(((s, j), (s, left), (s, right), (down, j), (up, j))):
        first = INDEX if at == 0 else INDEX + 12 + 4 * at
        for face in range(4):
            table_ref[first + face] = primal_ref[row, column, face]


def first_gather(
    face_len_ref, primal_ref, loads_ref, basis_ref, rows_ref, table_ref, o0, o1, o2, o3, terms_ref, hold_ref
):
    fill_table(table_ref, face_len_ref, primal_ref)
    spare = jnp.zeros((12, loads_ref.shape[1]), F32)
    x = jnp.concatenate([loads_ref[...], 0.5 * basis_ref[...], spare], axis=0)
    gather_slots(x, terms_ref, rows_ref, table_ref, hold_ref, (o0, o1, o2, o3))


def prepare(table_ref, rows_ref, matrix_at, weight_ref, inverse_ref, matrix_ref, terms_ref, sem):
    copy = pltpu.make_async_copy(matrix_at, matrix_ref, sem)
    copy.start()
    width = rows_ref.shape[1]
    face_width = width // 4
    row = lax.broadcasted_iota(jnp.int32, (16, face_width), 0)
    column = lax.broadcasted_iota(jnp.int32, (16, face_width), 1)
    for swap in range(4):
        slot = column + table_ref[FACE + swap] * face_width
        weight = 1.0 - 0.5 * (column < table_ref[swap]).astype(F32)
        extra = jnp.where(
            row == 0,
            weight,
            jnp.where(row == 1, (slot // 256).astype(F32), jnp.where(row == 2, (slot % 256).astype(F32), 0.0)),
        )
        terms_ref[:, face_columns(table_ref, swap, face_width)] = extra.astype(BF16)
    within = within_chunk(width)

    def one(chunk, carry):
        columns = pl.ds(pl.multiple_of(chunk * 256, 256), 256)
        hot = one_hot(rows_ref[...], chunk, within)
        y = lax.dot_general(terms_ref[...], hot, (((1,), (1,)), ((), ())), preferred_element_type=F32)
        weight_ref[:, columns] = y[0:1]
        inverse_ref[:, columns] = (y[1:2] * 256.0 + y[2:3]).astype(jnp.int32)
        return carry

    lax.fori_loop(0, width // 256, one, 0)
    copy.wait()


def first_scatter(
    table_ref, loads_ref, basis_ref, weight_ref, inverse_ref, i0, i1, i2, i3,
    residual_ref, weighted_ref, reach_ref, coarse_ref, terms_ref,
):
    block, width = loads_ref.shape
    face_width = width // 4
    row = lax.broadcasted_iota(jnp.int32, (16, face_width), 0)
    for swap, ref in enumerate((i0, i1, i2, i3)):
        face = table_ref[FACE + swap]
        got = ref[block : block + 4, :]
        spread = jnp.where(row // 4 == face, jnp.concatenate([got] * 4, axis=0), 0.0)
        both = jnp.concatenate([ref[0:block, :], spread], axis=0)
        put_terms(terms_ref, 0, slice(swap * face_width, (swap + 1) * face_width), three_terms(both))

    def gain(columns, y):
        residual = loads_ref[:, columns] + y[:block]
        weight = weight_ref[:, columns]
        residual_ref[:, columns] = residual
        weighted_ref[:, columns] = residual * weight
        blank = jnp.zeros((12, y.shape[1]), F32)
        reach = jnp.concatenate([weight * basis_ref[:, columns], blank, y[block:]], axis=0)
        put_terms(reach_ref, 0, columns, two_terms(reach))

    permute(terms_ref, inverse_ref, face_chunks(range(4), table_ref, face_width), gain)
    coarse = lax.dot_general(
        weighted_ref[...], basis_ref[...], (((1,), (1,)), ((), ())), precision=HIGH, preferred_element_type=F32
    )
    coarse_ref[...] = place(coarse, table_ref, range(4), coarse_ref.shape[1])


def first_sweep(begin, *refs):
    if begin:
        relax_ref, weighted_ref, matrix_ref, solve_ref, terms_ref = refs
        solve_ref[...] = relax_ref[0, 0] * weighted_ref[...]
    else:
        relax_ref, weighted_ref, matrix_ref, old_ref, solve_ref, terms_ref = refs
        solve_ref[...] = old_ref[...]
    sweep(weighted_ref, solve_ref, terms_ref, relax_ref[0, 0], matrix_ref)


def first_own(table_ref, solve_ref, weight_ref, rows_ref, own_ref, o0, o1, o2, o3, terms_ref, hold_ref):
    own_ref[...] = solve_ref[...] * weight_ref[...]
    gather_slots(own_ref[...], terms_ref, rows_ref, table_ref, hold_ref, (o0, o1, o2, o3))


def settle(first, start, *refs):
    refs = list(refs)
    solve_ref, weighted_ref, coarse_solution_ref, coarse_ref = refs[:4]
    rest = refs[4:]
    if start:
        coarse_inverse_ref = coarse_solution_ref
        rho_ref, coarse_rho_ref, coarse_solution_ref, left_ref, right_ref = rest
        coarse_solution_ref[...] = dot(coarse_ref[...], coarse_inverse_ref[...])
    else:
        whole_rho_ref, precond_ref, step_ref = rest[:3]
        rest = rest[3:]
        if not first:
            back_ref, old_direction_ref, old_solution_ref = rest[:3]
            rest = rest[3:]
        rho_ref, coarse_rho_ref, rho_inverse_ref, direction_ref, direction_terms_ref, solution_ref, left_ref, right_ref = rest
    put_terms(left_ref, 0, slice(None), three_terms(solve_ref[...]))
    put_terms(right_ref, 0, slice(None), three_terms(weighted_ref[...]))
    rho_ref[...] = gram(left_ref[...], right_ref[...], 3, 3)
    coarse_rho_ref[...] = lax.dot_general(
        coarse_solution_ref[...], coarse_ref[...], (((1,), (1,)), ((), ())), precision=HIGH, preferred_element_type=F32
    )
    if start:
        return
    n = whole_rho_ref.shape[0]
    row = lax.broadcasted_iota(jnp.int32, (n, n), 0)
    one = (row == lax.broadcasted_iota(jnp.int32, (n, n), 1)).astype(F32)
    rho_inverse_ref[...] = spd_solve(whole_rho_ref[...], one)
    step = stacked(step_ref[...])
    back = None if first else stacked(back_ref[...])

    def turn(columns, start_at, tile):
        direction = precond_ref[:, columns]
        if not first:
            direction = direction + mix(back, old_direction_ref[:, columns])
        direction_ref[:, columns] = direction
        put_terms(direction_terms_ref, 0, columns, three_terms(direction))
        moved = mix(step, direction)
        solution_ref[:, columns] = moved if first else old_solution_ref[:, columns] + moved

    over_columns(solve_ref.shape[1], 4, turn)


def apply_matrix(first, *refs):
    refs = list(refs)
    table_ref, own_ref, rho_ref, matrix_ref, reach_ref, inverse_ref = refs[:6]
    ins, rest = refs[6:10], refs[10:]
    if first:
        coarse_solution_ref = rest.pop(0)
    else:
        direction_terms_ref = rest.pop(0)
    precond_ref, partial_ref, sums_ref, terms_ref, more_ref = rest
    block = own_ref.shape[0]

    if first:
        width = coarse_solution_ref.shape[1]
        row = lax.broadcasted_iota(jnp.int32, (32, width), 0)
        at = lax.broadcasted_iota(jnp.int32, (32, width), 1)
        pick = jnp.zeros((32, width), F32)
        for member in MEMBERS:
            pick = jnp.where((row == member) & (at == table_ref[INDEX + member]), 1.0, pick)
        picked = lax.dot_general(
            coarse_solution_ref[...], pick, (((1,), (1,)), ((), ())), precision=HIGH, preferred_element_type=F32
        )
        picks = jnp.concatenate([jnp.concatenate([term] * 2, axis=1) for term in three_terms(picked)], axis=0)

    def gain(columns, y):
        precond = own_ref[:, columns] + y
        if first:
            precond = precond + fold(jnp.dot(picks, reach_ref[:, columns], preferred_element_type=F32), 3)
        precond_ref[:, columns] = precond

    scatter_faces(ins, range(4), terms_ref, inverse_ref, table_ref, gain)
    put_terms(terms_ref, 0, slice(None), three_terms(precond_ref[...]))
    put_terms(more_ref, 0, slice(None), two_terms(precond_ref[...]))

    def emit(columns, y):
        partial_ref[:, columns] = y

    product(more_ref.at[0 : 2 * block], matrix_ref, emit)
    put_terms(more_ref, 0, slice(None), three_terms(partial_ref[...]))
    partial = more_ref[...]
    sums_ref[:, 0:PLACE] = jnp.zeros((block, PLACE), F32)
    sums_ref[:, 0:block] = rho_ref[...]
    sums_ref[:, block : 2 * block] = gram(partial, terms_ref[...], 3, 3)
    if not first:
        sums_ref[:, 2 * block : 3 * block] = gram(partial, direction_terms_ref[...], 3, 3)
    coarse = gram(partial, reach_ref[...], 3, 2)
    sums_ref[:, PLACE:] = place(coarse, table_ref, MEMBERS, sums_ref.shape[1] - PLACE)


def gather_image(table_ref, partial_ref, rows_ref, o0, o1, o2, o3, terms_ref, hold_ref):
    gather_slots(partial_ref[...], terms_ref, rows_ref, table_ref, hold_ref, (o0, o1, o2, o3))


def scatter_image(table_ref, partial_ref, inverse_ref, i0, i1, i2, i3, image_ref, terms_ref):
    def gain(columns, y):
        image_ref[:, columns] = partial_ref[:, columns] + y

    scatter_faces((i0, i1, i2, i3), range(4), terms_ref, inverse_ref, table_ref, gain)


def advance(first, last, *refs):
    refs = list(refs)
    sums_ref, coarse_rho_ref, image_part_ref, residual_ref = refs[:4]
    rest = refs[4:]
    if not first:
        old_image_ref, old_curvature_ref, old_rho_inverse_ref = rest[:3]
        rest = rest[3:]
    if last:
        precond_ref, old_direction_ref, old_solution_ref, new_solution_ref, new_residual_ref = rest
    else:
        if not first:
            old_coarse_image_ref = rest.pop(0)
        table_ref, relax_ref, matrix_ref, weight_ref, basis_ref, rows_ref, coarse_ref, coarse_inverse_ref = rest[:8]
        rest = rest[8:]
        new_residual_ref, image_ref, curvature_ref, rho_out_ref, step_ref = rest[:5]
        rest = rest[5:]
        if not first:
            back_ref = rest.pop(0)
        coarse_image_ref, new_coarse_ref, coarse_solution_ref, solve_ref, weighted_ref, own_ref = rest[:6]
        o0, o1, o2, o3, terms_ref, hold_ref = rest[6:]
    block, width = residual_ref.shape
    rho = symmetric(sums_ref[:, 0:block] + coarse_rho_ref[...])
    curvature = symmetric(sums_ref[:, block : 2 * block])
    if not first:
        beta = dot(old_rho_inverse_ref[...], rho)
        back = beta.T
        cross = dot(sums_ref[:, 2 * block : 3 * block], beta)
        curvature = curvature + (cross + cross.T) + symmetric(dot(back, dot(old_curvature_ref[...], beta)))
        back_stack = stacked(back)
    step = spd_solve(curvature, rho).T
    step_stack = stacked(step)

    def one(columns, start, tile):
        image = image_part_ref[:, columns]
        if not first:
            image = image + mix(back_stack, old_image_ref[:, columns])
        residual = residual_ref[:, columns] - mix(step_stack, image)
        new_residual_ref[:, columns] = residual
        if last:
            direction = precond_ref[:, columns] + mix(back_stack, old_direction_ref[:, columns])
            new_solution_ref[:, columns] = old_solution_ref[:, columns] + mix(step_stack, direction)
        else:
            image_ref[:, columns] = image
            weighted = residual * weight_ref[:, columns]
            weighted_ref[:, columns] = weighted
            solve_ref[:, columns] = relax_ref[0, 0] * weighted

    over_columns(width, 4, one)
    if last:
        return
    step_ref[...] = step
    curvature_ref[...] = curvature
    rho_out_ref[...] = rho
    coarse_image = sums_ref[:, PLACE:]
    if not first:
        back_ref[...] = back
        coarse_image = coarse_image + dot(back, old_coarse_image_ref[...])
    coarse_image_ref[...] = coarse_image
    coarse = coarse_ref[...] - dot(step, coarse_image)
    new_coarse_ref[...] = coarse
    coarse_solution = dot(coarse, coarse_inverse_ref[...])
    coarse_solution_ref[...] = coarse_solution

    def again(t, carry):
        sweep(weighted_ref, solve_ref, terms_ref.at[0 : 2 * block], relax_ref[0, 0], matrix_ref)
        return carry

    lax.fori_loop(0, DEG, again, 0)
    own_ref[...] = correct(solve_ref, coarse_solution, table_ref, basis_ref, weight_ref)
    gather_slots(own_ref[...], terms_ref, rows_ref, table_ref, hold_ref, (o0, o1, o2, o3))


def on_core(kernel, args, scalars, outs, scratch, flops, far=(), scalar_outs=(), limit=12 * MIB):
    def spec(at, scalar, far):
        return pl.BlockSpec(memory_space=pltpu.SMEM if at in scalar else pltpu.HBM if at in far else pltpu.VMEM)

    size = sum(x.size * x.dtype.itemsize for x in args) + sum(4 * o.size for o in outs)
    return pl.pallas_call(
        kernel,
        out_shape=outs,
        in_specs=[spec(at, scalars, far) for at in range(len(args))],
        out_specs=[spec(at, scalar_outs, ()) for at in range(len(outs))],
        scratch_shapes=scratch,
        compiler_params=pltpu.CompilerParams(vmem_limit_bytes=limit),
        cost_estimate=pl.CostEstimate(flops=flops, bytes_accessed=size, transcendentals=0),
    )(*args)


def swap(x, axis, partner):
    return lax.ppermute(x, axis, [(i, partner(i)) for i in range(lax.axis_size(axis))])


def exchange(slots):
    subs, segs = lax.axis_size("sub"), lax.axis_size("seg")
    inner = [(i, ((i - 1) ^ 1) + 1) for i in range(1, segs - 1)]
    return [
        swap(slots[0], "sub", lambda i: i ^ 1),
        swap(slots[1], "sub", lambda i: (((i - 1) % subs ^ 1) + 1) % subs),
        swap(slots[2], "seg", lambda i: i ^ 1),
        lax.ppermute(slots[3], "seg", inner),
    ]


def ring_swaps(x, axis, stride):
    return [swap(x, axis, lambda i, k=k: i ^ (k * stride)) for k in (1, 2, 3)]


def beside(work, *others):
    return lax.optimization_barrier((work, *others))


def add_all(x, parts):
    return (x + parts[0]) + (parts[1] + parts[2])


def body(nodal_loads, schur_matrix, face_rows, face_len, relax_step, coarse_basis, primal_index, coarse_inverse):
    loads, matrix, rows, basis = nodal_loads[0, 0], schur_matrix[0, 0], face_rows[0], coarse_basis[0, 0]
    block, width = loads.shape
    face_width = width // 4
    coarse_count = coarse_inverse.shape[0]

    shape = lambda *size: jax.ShapeDtypeStruct(size, F32)
    full, small, coarse_block = shape(block, width), shape(block, block), shape(block, coarse_count)
    terms = pltpu.VMEM((3 * block, width), BF16)
    hold = pltpu.VMEM((block, width), F32)
    faces = [shape(block, face_width)] * 4
    move = 2 * 3 * block * width * width
    turn = 2 * 2 * block * width * width
    light = 2 * 9 * block * block * width

    wide = [shape(block + 8, face_width)] * 4
    ints = lambda *size: jax.ShapeDtypeStruct(size, jnp.int32)
    table, *slots = on_core(
        first_gather, (face_len, primal_index, loads, basis, rows), (0, 1), [ints(INDEX + 32), *wide],
        [pltpu.VMEM((3 * (block + 16), width), BF16), pltpu.VMEM((block + 16, width), F32)], move, scalar_outs=(0,),
    )
    got = exchange(slots)
    weight, inverse, matrix = on_core(
        prepare, (table, rows, matrix), (0,), [shape(1, width), ints(1, width), jax.ShapeDtypeStruct((width, width), BF16)],
        [pltpu.VMEM((16, width), BF16), pltpu.SemaphoreType.DMA], move, far=(2,), limit=30 * MIB,
    )
    weight, *got = beside(weight, *got)
    residual, weighted, reach, coarse = on_core(
        first_scatter, (table, loads, basis, weight, inverse, *got), (0,),
        [full, full, jax.ShapeDtypeStruct((64, width), BF16), coarse_block],
        [pltpu.VMEM((3 * (block + 16), width), BF16)], move,
    )
    half_terms = pltpu.VMEM((2 * block, width), BF16)

    def one_sweep(*old):
        return on_core(
            functools.partial(first_sweep, not old), (relax_step, weighted, matrix, *old), (0,), [full], [half_terms], turn,
        )[0]

    part = swap(coarse, "seg", lambda i: i ^ 1)
    solve, part = beside(one_sweep(), part)
    coarse = coarse + part
    parts = ring_swaps(coarse, "seg", 2)
    solve, *parts = beside(one_sweep(solve), *parts)
    coarse = add_all(coarse, parts)
    parts = ring_swaps(coarse, "sub", 1)
    solve = one_sweep(solve)
    own, *slots = on_core(first_own, (table, solve, weight, rows), (0,), [full, *faces], [terms, hold], move)
    own, *parts = beside(own, *parts)
    coarse = add_all(coarse, parts)
    three = jax.ShapeDtypeStruct((3 * block, width), BF16)
    step = back = precond = coarse_solution = direction = image = answer = curvature = rho = coarse_image = None
    for iteration in range(ITERS):
        first, last = iteration == 0, iteration + 1 == ITERS
        if first:
            parts = ring_swaps(coarse, "sub", 4)
        got = exchange(slots)
        if first:
            coarse = add_all(coarse, parts)
        settled = [solve, weighted, coarse_inverse if first else coarse_solution, coarse]
        outs = [small, small] + ([coarse_block] if first else [])
        if iteration:
            settled += [rho, precond, step] + ([back, direction, answer] if iteration > 1 else [])
            outs += [small, full, three, full]
        settled = on_core(
            functools.partial(settle, iteration == 1, first), settled, (), outs, [terms, terms], light,
        )
        local_rho, *got = beside(settled[0], *got)
        coarse_rho = settled[1]
        if first:
            coarse_solution = settled[2]
        else:
            rho_inverse, direction, direction_terms, answer = settled[2:]
        precond, partial, sums = on_core(
            functools.partial(apply_matrix, first),
            (table, own, local_rho, matrix, reach, inverse, *got, coarse_solution if first else direction_terms), (0,),
            [full, full, shape(block, PLACE + coarse_count)], [terms, terms], turn + move,
        )
        part = swap(sums, "seg", lambda i: i ^ 1)
        slots = on_core(gather_image, (table, partial, rows), (0,), faces, [terms, hold], move)
        part, *slots = beside(part, *slots)
        sums = sums + part
        parts = ring_swaps(sums, "seg", 2)
        got = exchange(slots)
        sums = add_all(sums, parts)
        sums, got[0], got[2], got[3] = beside(sums, got[0], got[2], got[3])
        parts = ring_swaps(sums, "sub", 1)
        got[1], *parts = beside(got[1], *parts)
        sums = add_all(sums, parts)
        parts = ring_swaps(sums, "sub", 4)
        image_part, = on_core(scatter_image, (table, partial, inverse, *got), (0,), [full], [terms], move)
        image_part, *parts = beside(image_part, *parts)
        args = [coarse_rho, image_part, residual]
        if not first:
            args += [image, curvature, rho_inverse]
        args = [add_all(sums, parts), *args]
        if last:
            answer, residual = on_core(
                functools.partial(advance, first, last), (*args, precond, direction, answer), (), [full, full], [], light,
            )
            break
        if not first:
            args += [coarse_image]
        at = len(args)
        args += [table, relax_step, matrix, weight, basis, rows, coarse, coarse_inverse]
        outs = [full, full, small, small, small] + ([] if first else [small])
        outs += [coarse_block, coarse_block, coarse_block, full, full, full, *faces]
        residual, image, curvature, rho, step, *rest = on_core(
            functools.partial(advance, first, last), args, (at, at + 1), outs, [terms, hold], 3 * turn + move,
        )
        if not first:
            back = rest.pop(0)
        coarse_image, coarse, coarse_solution, solve, weighted, own, *slots = rest
    return (answer[None, None], residual[None, None])


def solution(mesh):
    placed = (
        P("seg", "sub", None, None),
        P("seg", "sub", None, None),
        P("seg", "sub", None),
        P(),
        P("seg", "sub"),
        P("seg", "sub", None, None),
        P(),
        P(),
    )
    return jax.shard_map(
        body,
        mesh=mesh,
        in_specs=placed,
        out_specs=(P("seg", "sub", None, None), P("seg", "sub", None, None)),
        check_vma=False,
    )
```

```python
import functools

import jax
import jax.numpy as jnp
from jax import lax
from jax.experimental import pallas as pl
from jax.experimental.pallas import tpu as pltpu
from jax.sharding import PartitionSpec as P

DEG = 3
ITERS = 3
HIGH = lax.Precision.HIGHEST
F32 = jnp.float32
BF16 = jnp.bfloat16
MIB = 1 << 20

PLACE = 128
FACE = 4
INDEX = 8
MEMBERS = (0, 1, 2, 3) + tuple(range(16, 32))


def dot(a, b):
    return jnp.dot(a, b, precision=HIGH, preferred_element_type=F32)


def symmetric(matrix):
    return 0.5 * (matrix + matrix.T)


def two_terms(x):
    hi = x.astype(BF16)
    return hi, (x - hi.astype(F32)).astype(BF16)


def three_terms(x):
    hi = x.astype(BF16)
    rest = x - hi.astype(F32)
    mid = rest.astype(BF16)
    return hi, mid, (rest - mid.astype(F32)).astype(BF16)


def put_terms(ref, first, columns, terms):
    rows = terms[0].shape[0]
    for at, term in enumerate(terms):
        ref[first + at * rows : first + (at + 1) * rows, columns] = term


def fold(y, parts):
    rows = y.shape[0] // parts
    total = y[:rows]
    for at in range(1, parts):
        total = total + y[at * rows : (at + 1) * rows]
    return total


def gram(left, right, left_parts, right_parts):
    y = lax.dot_general(left, right, (((1,), (1,)), ((), ())), preferred_element_type=F32)
    y = fold(y, left_parts)
    columns = y.shape[1] // right_parts
    total = y[:, :columns]
    for at in range(1, right_parts):
        total = total + y[:, at * columns : (at + 1) * columns]
    return total


def stacked(matrix):
    return jnp.concatenate([jnp.concatenate([term] * 3, axis=1) for term in three_terms(matrix)], axis=0)


def mix(stack, x):
    terms = jnp.concatenate(three_terms(x), axis=0)
    return fold(jnp.dot(stack, terms, preferred_element_type=F32), 3)


def cut(width, parts):
    return width // parts if width % parts == 0 and (width // parts) % 128 == 0 else width // 4


def over_columns(width, parts, one):
    tile = cut(width, parts)

    def step(t, carry):
        start = pl.multiple_of(t * tile, tile)
        one(pl.ds(start, tile), start, tile)
        return carry

    lax.fori_loop(0, width // tile, step, 0)


def spd_solve(a, b):
    n, block = a.shape[0], 8
    both = jnp.concatenate([a, b], axis=1)
    row = lax.broadcasted_iota(jnp.int32, (n, 1), 0)
    for k in range(0, n, block):
        columns = [jnp.broadcast_to(both[:, k + j : k + j + 1], both.shape) for j in range(block)]
        rows = [both[k + i : k + i + 1, :] for i in range(block)]
        small = [[columns[j][k + i : k + i + 1, :] for j in range(block)] for i in range(block)]
        for p in range(block):
            over = 1.0 / small[p][p]
            rows[p] = rows[p] * over
            for j in range(p + 1, block):
                small[p][j] = small[p][j] * over
            for i in range(block):
                if i != p:
                    rows[i] = rows[i] - small[i][p] * rows[p]
                    for j in range(p + 1, block):
                        small[i][j] = small[i][j] - small[i][p] * small[p][j]
        after = both
        for j in range(block):
            after = after - columns[j] * rows[j]
        for j in range(block):
            after = jnp.where(row == k + j, rows[j], after)
        both = after
    return both[:, n:]


def one_hot(index, chunk, within):
    low = jnp.where(index // 256 == chunk, (index % 256).astype(F32), -1.0).astype(BF16)
    return jnp.where(within == low, jnp.ones((), BF16), jnp.zeros((), BF16))


def within_chunk(columns):
    return lax.broadcasted_iota(jnp.int32, (256, columns), 0).astype(F32).astype(BF16)


def permute(terms_ref, index_ref, chunks, emit):
    within = within_chunk(cut(index_ref.shape[1], 4))

    def one(columns, start, tile):
        index = index_ref[0:1, columns]
        y = None
        for at, chunk in enumerate(chunks):
            hot = one_hot(index, chunk, within)
            part = jnp.dot(terms_ref[:, at * 256 : (at + 1) * 256], hot, preferred_element_type=F32)
            y = part if y is None else y + part
        emit(columns, fold(y, 3))

    over_columns(index_ref.shape[1], 4, one)


def face_columns(table_ref, swap, face_width):
    return pl.ds(pl.multiple_of(table_ref[FACE + swap] * face_width, face_width), face_width)


def gather_slots(x, terms_ref, rows_ref, table_ref, hold_ref, out_refs):
    put_terms(terms_ref, 0, slice(None), three_terms(x))

    def emit(columns, y):
        hold_ref[:, columns] = y

    permute(terms_ref, rows_ref, range(rows_ref.shape[1] // 256), emit)
    face_width = rows_ref.shape[1] // 4
    at = lax.broadcasted_iota(jnp.int32, (1, face_width), 1)
    for swap, out in enumerate(out_refs):
        part = hold_ref[0 : out.shape[0], face_columns(table_ref, swap, face_width)]
        out[...] = part * (at < table_ref[swap]).astype(F32)


def face_chunks(swaps, table_ref, face_width):
    each = face_width // 256
    return [table_ref[FACE + swap] * each + part for swap in swaps for part in range(each)]


def scatter_faces(in_refs, swaps, terms_ref, inverse_ref, table_ref, emit):
    face_width = inverse_ref.shape[1] // 4
    for at, ref in enumerate(in_refs):
        put_terms(terms_ref, 0, slice(at * face_width, (at + 1) * face_width), three_terms(ref[...]))
    permute(terms_ref, inverse_ref, face_chunks(swaps, table_ref, face_width), emit)


def product(terms_ref, matrix_ref, emit):
    def one(columns, start, tile):
        emit(columns, fold(jnp.dot(terms_ref[...], matrix_ref[:, columns], preferred_element_type=F32), 2))

    over_columns(matrix_ref.shape[1], 3, one)


def sweep(weighted_ref, solve_ref, terms_ref, relax, matrix_ref):
    put_terms(terms_ref, 0, slice(None), two_terms(solve_ref[...]))

    def emit(columns, y):
        solve_ref[:, columns] = relax * weighted_ref[:, columns] + solve_ref[:, columns] - relax * y

    product(terms_ref, matrix_ref, emit)


def place(columns, table_ref, members, width):
    at = lax.broadcasted_iota(jnp.int32, (1, width), 1)
    total = jnp.zeros((columns.shape[0], width), F32)
    for member in members:
        total = total + columns[:, member : member + 1] * (at == table_ref[INDEX + member]).astype(F32)
    return total


def correct(solve_ref, coarse_solution, table_ref, basis_ref, weight_ref):
    at = lax.broadcasted_iota(jnp.int32, (1, coarse_solution.shape[1]), 1)
    solve = solve_ref[...]
    for face in range(4):
        mine = (at == table_ref[INDEX + face]).astype(F32)
        picked = jnp.sum(coarse_solution * mine, axis=1, keepdims=True)
        solve = solve + picked * basis_ref[face : face + 1, :]
    return solve * weight_ref[...]


def fill_table(table_ref, face_len_ref, primal_ref):
    s, j = lax.axis_index("seg"), lax.axis_index("sub")
    segs, subs = face_len_ref.shape[:2]
    left, right = lax.rem(j + subs - 1, subs), lax.rem(j + 1, subs)
    down, up = jnp.maximum(s - 1, 0), jnp.minimum(s + 1, segs - 1)
    sub_odd, seg_odd = lax.rem(j, 2), lax.rem(s, 2)
    lengths = (
        face_len_ref[s, left, 0],
        face_len_ref[s, j, 0],
        jnp.where(s > 0, face_len_ref[down, j, 1], 0),
        jnp.where(s < segs - 1, face_len_ref[s, j, 1], 0),
    )
    table_ref[0] = jnp.where(sub_odd == 0, lengths[1], lengths[0])
    table_ref[1] = jnp.where(sub_odd == 0, lengths[0], lengths[1])
    table_ref[2] = jnp.where(seg_odd == 0, lengths[3], lengths[2])
    table_ref[3] = jnp.where(seg_odd == 0, lengths[2], lengths[3])
    table_ref[FACE] = 1 - sub_odd
    table_ref[FACE + 1] = sub_odd
    table_ref[FACE + 2] = 3 - seg_odd
    table_ref[FACE + 3] = 2 + seg_odd
    for at, (row, column) in enumerate(((s, j), (s, left), (s, right), (down, j), (up, j))):
        first = INDEX if at == 0 else INDEX + 12 + 4 * at
        for face in range(4):
            table_ref[first + face] = primal_ref[row, column, face]


def first_gather(
    face_len_ref, primal_ref, loads_ref, basis_ref, rows_ref, table_ref, o0, o1, o2, o3, terms_ref, hold_ref
):
    fill_table(table_ref, face_len_ref, primal_ref)
    spare = jnp.zeros((12, loads_ref.shape[1]), F32)
    x = jnp.concatenate([loads_ref[...], 0.5 * basis_ref[...], spare], axis=0)
    gather_slots(x, terms_ref, rows_ref, table_ref, hold_ref, (o0, o1, o2, o3))


def prepare(table_ref, rows_ref, matrix_at, weight_ref, inverse_ref, matrix_ref, terms_ref, sem):
    copy = pltpu.make_async_copy(matrix_at, matrix_ref, sem)
    copy.start()
    width = rows_ref.shape[1]
    face_width = width // 4
    row = lax.broadcasted_iota(jnp.int32, (16, face_width), 0)
    column = lax.broadcasted_iota(jnp.int32, (16, face_width), 1)
    for swap in range(4):
        slot = column + table_ref[FACE + swap] * face_width
        weight = 1.0 - 0.5 * (column < table_ref[swap]).astype(F32)
        extra = jnp.where(
            row == 0,
            weight,
            jnp.where(row == 1, (slot // 256).astype(F32), jnp.where(row == 2, (slot % 256).astype(F32), 0.0)),
        )
        terms_ref[:, face_columns(table_ref, swap, face_width)] = extra.astype(BF16)
    within = within_chunk(width)

    def one(chunk, carry):
        columns = pl.ds(pl.multiple_of(chunk * 256, 256), 256)
        hot = one_hot(rows_ref[...], chunk, within)
        y = lax.dot_general(terms_ref[...], hot, (((1,), (1,)), ((), ())), preferred_element_type=F32)
        weight_ref[:, columns] = y[0:1]
        inverse_ref[:, columns] = (y[1:2] * 256.0 + y[2:3]).astype(jnp.int32)
        return carry

    lax.fori_loop(0, width // 256, one, 0)
    copy.wait()


def first_scatter(
    table_ref, loads_ref, basis_ref, weight_ref, inverse_ref, i0, i1, i2, i3,
    residual_ref, weighted_ref, reach_ref, coarse_ref, terms_ref,
):
    block, width = loads_ref.shape
    face_width = width // 4
    row = lax.broadcasted_iota(jnp.int32, (16, face_width), 0)
    for swap, ref in enumerate((i0, i1, i2, i3)):
        face = table_ref[FACE + swap]
        got = ref[block : block + 4, :]
        spread = jnp.where(row // 4 == face, jnp.concatenate([got] * 4, axis=0), 0.0)
        both = jnp.concatenate([ref[0:block, :], spread], axis=0)
        put_terms(terms_ref, 0, slice(swap * face_width, (swap + 1) * face_width), three_terms(both))

    def gain(columns, y):
        residual = loads_ref[:, columns] + y[:block]
        weight = weight_ref[:, columns]
        residual_ref[:, columns] = residual
        weighted_ref[:, columns] = residual * weight
        blank = jnp.zeros((12, y.shape[1]), F32)
        reach = jnp.concatenate([weight * basis_ref[:, columns], blank, y[block:]], axis=0)
        put_terms(reach_ref, 0, columns, two_terms(reach))

    permute(terms_ref, inverse_ref, face_chunks(range(4), table_ref, face_width), gain)
    coarse = lax.dot_general(
        weighted_ref[...], basis_ref[...], (((1,), (1,)), ((), ())), precision=HIGH, preferred_element_type=F32
    )
    coarse_ref[...] = place(coarse, table_ref, range(4), coarse_ref.shape[1])


def first_sweep(begin, *refs):
    if begin:
        relax_ref, weighted_ref, matrix_ref, solve_ref, terms_ref = refs
        solve_ref[...] = relax_ref[0, 0] * weighted_ref[...]
    else:
        relax_ref, weighted_ref, matrix_ref, old_ref, solve_ref, terms_ref = refs
        solve_ref[...] = old_ref[...]
    sweep(weighted_ref, solve_ref, terms_ref, relax_ref[0, 0], matrix_ref)


def first_own(table_ref, solve_ref, weight_ref, rows_ref, own_ref, o0, o1, o2, o3, terms_ref, hold_ref):
    own_ref[...] = solve_ref[...] * weight_ref[...]
    gather_slots(own_ref[...], terms_ref, rows_ref, table_ref, hold_ref, (o0, o1, o2, o3))


def settle(first, start, *refs):
    refs = list(refs)
    solve_ref, weighted_ref, coarse_solution_ref, coarse_ref = refs[:4]
    rest = refs[4:]
    if start:
        coarse_inverse_ref = coarse_solution_ref
        rho_ref, coarse_rho_ref, coarse_solution_ref, left_ref, right_ref = rest
        coarse_solution_ref[...] = dot(coarse_ref[...], coarse_inverse_ref[...])
    else:
        whole_rho_ref, precond_ref, step_ref = rest[:3]
        rest = rest[3:]
        if not first:
            back_ref, old_direction_ref, old_solution_ref = rest[:3]
            rest = rest[3:]
        rho_ref, coarse_rho_ref, rho_inverse_ref, direction_ref, direction_terms_ref, solution_ref, left_ref, right_ref = rest
    put_terms(left_ref, 0, slice(None), three_terms(solve_ref[...]))
    put_terms(right_ref, 0, slice(None), three_terms(weighted_ref[...]))
    rho_ref[...] = gram(left_ref[...], right_ref[...], 3, 3)
    coarse_rho_ref[...] = lax.dot_general(
        coarse_solution_ref[...], coarse_ref[...], (((1,), (1,)), ((), ())), precision=HIGH, preferred_element_type=F32
    )
    if start:
        return
    n = whole_rho_ref.shape[0]
    row = lax.broadcasted_iota(jnp.int32, (n, n), 0)
    one = (row == lax.broadcasted_iota(jnp.int32, (n, n), 1)).astype(F32)
    rho_inverse_ref[...] = spd_solve(whole_rho_ref[...], one)
    step = stacked(step_ref[...])
    back = None if first else stacked(back_ref[...])

    def turn(columns, start_at, tile):
        direction = precond_ref[:, columns]
        if not first:
            direction = direction + mix(back, old_direction_ref[:, columns])
        direction_ref[:, columns] = direction
        put_terms(direction_terms_ref, 0, columns, three_terms(direction))
        moved = mix(step, direction)
        solution_ref[:, columns] = moved if first else old_solution_ref[:, columns] + moved

    over_columns(solve_ref.shape[1], 4, turn)


def apply_matrix(first, *refs):
    refs = list(refs)
    table_ref, own_ref, rho_ref, matrix_ref, reach_ref, inverse_ref = refs[:6]
    ins, rest = refs[6:10], refs[10:]
    if first:
        coarse_solution_ref = rest.pop(0)
    else:
        direction_terms_ref = rest.pop(0)
    precond_ref, partial_ref, sums_ref, terms_ref, more_ref = rest
    block = own_ref.shape[0]

    if first:
        width = coarse_solution_ref.shape[1]
        row = lax.broadcasted_iota(jnp.int32, (32, width), 0)
        at = lax.broadcasted_iota(jnp.int32, (32, width), 1)
        pick = jnp.zeros((32, width), F32)
        for member in MEMBERS:
            pick = jnp.where((row == member) & (at == table_ref[INDEX + member]), 1.0, pick)
        picked = lax.dot_general(
            coarse_solution_ref[...], pick, (((1,), (1,)), ((), ())), precision=HIGH, preferred_element_type=F32
        )
        picks = jnp.concatenate([jnp.concatenate([term] * 2, axis=1) for term in three_terms(picked)], axis=0)

    def gain(columns, y):
        precond = own_ref[:, columns] + y
        if first:
            precond = precond + fold(jnp.dot(picks, reach_ref[:, columns], preferred_element_type=F32), 3)
        precond_ref[:, columns] = precond

    scatter_faces(ins, range(4), terms_ref, inverse_ref, table_ref, gain)
    put_terms(terms_ref, 0, slice(None), three_terms(precond_ref[...]))
    put_terms(more_ref, 0, slice(None), two_terms(precond_ref[...]))

    def emit(columns, y):
        partial_ref[:, columns] = y

    product(more_ref.at[0 : 2 * block], matrix_ref, emit)
    put_terms(more_ref, 0, slice(None), three_terms(partial_ref[...]))
    partial = more_ref[...]
    sums_ref[:, 0:PLACE] = jnp.zeros((block, PLACE), F32)
    sums_ref[:, 0:block] = rho_ref[...]
    sums_ref[:, block : 2 * block] = gram(partial, terms_ref[...], 3, 3)
    if not first:
        sums_ref[:, 2 * block : 3 * block] = gram(partial, direction_terms_ref[...], 3, 3)
    coarse = gram(partial, reach_ref[...], 3, 2)
    sums_ref[:, PLACE:] = place(coarse, table_ref, MEMBERS, sums_ref.shape[1] - PLACE)


def gather_image(table_ref, partial_ref, rows_ref, o0, o1, o2, o3, terms_ref, hold_ref):
    gather_slots(partial_ref[...], terms_ref, rows_ref, table_ref, hold_ref, (o0, o1, o2, o3))


def scatter_image(table_ref, partial_ref, inverse_ref, i0, i1, i2, i3, image_ref, terms_ref):
    def gain(columns, y):
        image_ref[:, columns] = partial_ref[:, columns] + y

    scatter_faces((i0, i1, i2, i3), range(4), terms_ref, inverse_ref, table_ref, gain)


def advance(first, last, *refs):
    refs = list(refs)
    sums_ref, coarse_rho_ref, image_part_ref, residual_ref = refs[:4]
    rest = refs[4:]
    if not first:
        old_image_ref, old_curvature_ref, old_rho_inverse_ref = rest[:3]
        rest = rest[3:]
    if last:
        precond_ref, old_direction_ref, old_solution_ref, new_solution_ref, new_residual_ref = rest
    else:
        if not first:
            old_coarse_image_ref = rest.pop(0)
        table_ref, relax_ref, matrix_ref, weight_ref, basis_ref, rows_ref, coarse_ref, coarse_inverse_ref = rest[:8]
        rest = rest[8:]
        new_residual_ref, image_ref, curvature_ref, rho_out_ref, step_ref = rest[:5]
        rest = rest[5:]
        if not first:
            back_ref = rest.pop(0)
        coarse_image_ref, new_coarse_ref, coarse_solution_ref, solve_ref, weighted_ref, own_ref = rest[:6]
        o0, o1, o2, o3, terms_ref, hold_ref = rest[6:]
    block, width = residual_ref.shape
    rho = symmetric(sums_ref[:, 0:block] + coarse_rho_ref[...])
    curvature = symmetric(sums_ref[:, block : 2 * block])
    if not first:
        beta = dot(old_rho_inverse_ref[...], rho)
        back = beta.T
        cross = dot(sums_ref[:, 2 * block : 3 * block], beta)
        curvature = curvature + (cross + cross.T) + symmetric(dot(back, dot(old_curvature_ref[...], beta)))
        back_stack = stacked(back)
    step = spd_solve(curvature, rho).T
    step_stack = stacked(step)

    def one(columns, start, tile):
        image = image_part_ref[:, columns]
        if not first:
            image = image + mix(back_stack, old_image_ref[:, columns])
        residual = residual_ref[:, columns] - mix(step_stack, image)
        new_residual_ref[:, columns] = residual
        if last:
            direction = precond_ref[:, columns] + mix(back_stack, old_direction_ref[:, columns])
            new_solution_ref[:, columns] = old_solution_ref[:, columns] + mix(step_stack, direction)
        else:
            image_ref[:, columns] = image
            weighted = residual * weight_ref[:, columns]
            weighted_ref[:, columns] = weighted
            solve_ref[:, columns] = relax_ref[0, 0] * weighted

    over_columns(width, 4, one)
    if last:
        return
    step_ref[...] = step
    curvature_ref[...] = curvature
    rho_out_ref[...] = rho
    coarse_image = sums_ref[:, PLACE:]
    if not first:
        back_ref[...] = back
        coarse_image = coarse_image + dot(back, old_coarse_image_ref[...])
    coarse_image_ref[...] = coarse_image
    coarse = coarse_ref[...] - dot(step, coarse_image)
    new_coarse_ref[...] = coarse
    coarse_solution = dot(coarse, coarse_inverse_ref[...])
    coarse_solution_ref[...] = coarse_solution

    def again(t, carry):
        sweep(weighted_ref, solve_ref, terms_ref.at[0 : 2 * block], relax_ref[0, 0], matrix_ref)
        return carry

    lax.fori_loop(0, DEG, again, 0)
    own_ref[...] = correct(solve_ref, coarse_solution, table_ref, basis_ref, weight_ref)
    gather_slots(own_ref[...], terms_ref, rows_ref, table_ref, hold_ref, (o0, o1, o2, o3))


def on_core(kernel, args, scalars, outs, scratch, flops, far=(), scalar_outs=(), limit=12 * MIB):
    def spec(at, scalar, far):
        return pl.BlockSpec(memory_space=pltpu.SMEM if at in scalar else pltpu.HBM if at in far else pltpu.VMEM)

    size = sum(x.size * x.dtype.itemsize for x in args) + sum(4 * o.size for o in outs)
    return pl.pallas_call(
        kernel,
        out_shape=outs,
        in_specs=[spec(at, scalars, far) for at in range(len(args))],
        out_specs=[spec(at, scalar_outs, ()) for at in range(len(outs))],
        scratch_shapes=scratch,
        compiler_params=pltpu.CompilerParams(vmem_limit_bytes=limit),
        cost_estimate=pl.CostEstimate(flops=flops, bytes_accessed=size, transcendentals=0),
    )(*args)


def swap(x, axis, partner):
    return lax.ppermute(x, axis, [(i, partner(i)) for i in range(lax.axis_size(axis))])


def exchange(slots):
    subs, segs = lax.axis_size("sub"), lax.axis_size("seg")
    inner = [(i, ((i - 1) ^ 1) + 1) for i in range(1, segs - 1)]
    return [
        swap(slots[0], "sub", lambda i: i ^ 1),
        swap(slots[1], "sub", lambda i: (((i - 1) % subs ^ 1) + 1) % subs),
        swap(slots[2], "seg", lambda i: i ^ 1),
        lax.ppermute(slots[3], "seg", inner),
    ]


def ring_swaps(x, axis, stride):
    return [swap(x, axis, lambda i, k=k: i ^ (k * stride)) for k in (1, 2, 3)]


def beside(work, *others):
    return lax.optimization_barrier((work, *others))


def add_all(x, parts):
    return (x + parts[0]) + (parts[1] + parts[2])


def body(nodal_loads, schur_matrix, face_rows, face_len, relax_step, coarse_basis, primal_index, coarse_inverse):
    loads, matrix, rows, basis = nodal_loads[0, 0], schur_matrix[0, 0], face_rows[0], coarse_basis[0, 0]
    block, width = loads.shape
    face_width = width // 4
    coarse_count = coarse_inverse.shape[0]

    shape = lambda *size: jax.ShapeDtypeStruct(size, F32)
    full, small, coarse_block = shape(block, width), shape(block, block), shape(block, coarse_count)
    terms = pltpu.VMEM((3 * block, width), BF16)
    hold = pltpu.VMEM((block, width), F32)
    faces = [shape(block, face_width)] * 4
    move = 2 * 3 * block * width * width
    turn = 2 * 2 * block * width * width
    light = 2 * 9 * block * block * width

    wide = [shape(block + 8, face_width)] * 4
    ints = lambda *size: jax.ShapeDtypeStruct(size, jnp.int32)
    table, *slots = on_core(
        first_gather, (face_len, primal_index, loads, basis, rows), (0, 1), [ints(INDEX + 32), *wide],
        [pltpu.VMEM((3 * (block + 16), width), BF16), pltpu.VMEM((block + 16, width), F32)], move, scalar_outs=(0,),
    )
    got = exchange(slots)
    weight, inverse, matrix = on_core(
        prepare, (table, rows, matrix), (0,), [shape(1, width), ints(1, width), jax.ShapeDtypeStruct((width, width), BF16)],
        [pltpu.VMEM((16, width), BF16), pltpu.SemaphoreType.DMA], move, far=(2,), limit=30 * MIB,
    )
    weight, *got = beside(weight, *got)
    residual, weighted, reach, coarse = on_core(
        first_scatter, (table, loads, basis, weight, inverse, *got), (0,),
        [full, full, jax.ShapeDtypeStruct((64, width), BF16), coarse_block],
        [pltpu.VMEM((3 * (block + 16), width), BF16)], move,
    )
    half_terms = pltpu.VMEM((2 * block, width), BF16)

    def one_sweep(*old):
        return on_core(
            functools.partial(first_sweep, not old), (relax_step, weighted, matrix, *old), (0,), [full], [half_terms], turn,
        )[0]

    part = swap(coarse, "seg", lambda i: i ^ 1)
    solve, part = beside(one_sweep(), part)
    coarse = coarse + part
    parts = ring_swaps(coarse, "seg", 2)
    solve, *parts = beside(one_sweep(solve), *parts)
    coarse = add_all(coarse, parts)
    parts = ring_swaps(coarse, "sub", 1)
    solve = one_sweep(solve)
    own, *slots = on_core(first_own, (table, solve, weight, rows), (0,), [full, *faces], [terms, hold], move)
    own, *parts = beside(own, *parts)
    coarse = add_all(coarse, parts)
    three = jax.ShapeDtypeStruct((3 * block, width), BF16)
    step = back = precond = coarse_solution = direction = image = answer = curvature = rho = coarse_image = None
    for iteration in range(ITERS):
        first, last = iteration == 0, iteration + 1 == ITERS
        if first:
            parts = ring_swaps(coarse, "sub", 4)
        got = exchange(slots)
        if first:
            coarse = add_all(coarse, parts)
        settled = [solve, weighted, coarse_inverse if first else coarse_solution, coarse]
        outs = [small, small] + ([coarse_block] if first else [])
        if iteration:
            settled += [rho, precond, step] + ([back, direction, answer] if iteration > 1 else [])
            outs += [small, full, three, full]
        settled = on_core(
            functools.partial(settle, iteration == 1, first), settled, (), outs, [terms, terms], light,
        )
        local_rho, *got = beside(settled[0], *got)
        coarse_rho = settled[1]
        if first:
            coarse_solution = settled[2]
        else:
            rho_inverse, direction, direction_terms, answer = settled[2:]
        precond, partial, sums = on_core(
            functools.partial(apply_matrix, first),
            (table, own, local_rho, matrix, reach, inverse, *got, coarse_solution if first else direction_terms), (0,),
            [full, full, shape(block, PLACE + coarse_count)], [terms, terms], turn + move,
        )
        part = swap(sums, "seg", lambda i: i ^ 1)
        slots = on_core(gather_image, (table, partial, rows), (0,), faces, [terms, hold], move)
        part, *slots = beside(part, *slots)
        sums = sums + part
        parts = ring_swaps(sums, "sub", 4)
        got = exchange(slots)
        sums = add_all(sums, parts)
        sums, got[0], got[2], got[3] = beside(sums, got[0], got[2], got[3])
        parts = ring_swaps(sums, "seg", 2)
        got[1], *parts = beside(got[1], *parts)
        sums = add_all(sums, parts)
        parts = ring_swaps(sums, "sub", 1)
        image_part, = on_core(scatter_image, (table, partial, inverse, *got), (0,), [full], [terms], move)
        image_part, *parts = beside(image_part, *parts)
        args = [coarse_rho, image_part, residual]
        if not first:
            args += [image, curvature, rho_inverse]
        args = [add_all(sums, parts), *args]
        if last:
            answer, residual = on_core(
                functools.partial(advance, first, last), (*args, precond, direction, answer), (), [full, full], [], light,
            )
            break
        if not first:
            args += [coarse_image]
        at = len(args)
        args += [table, relax_step, matrix, weight, basis, rows, coarse, coarse_inverse]
        outs = [full, full, small, small, small] + ([] if first else [small])
        outs += [coarse_block, coarse_block, coarse_block, full, full, full, *faces]
        residual, image, curvature, rho, step, *rest = on_core(
            functools.partial(advance, first, last), args, (at, at + 1), outs, [terms, hold], 3 * turn + move,
        )
        if not first:
            back = rest.pop(0)
        coarse_image, coarse, coarse_solution, solve, weighted, own, *slots = rest
    return (answer[None, None], residual[None, None])


def solution(mesh):
    placed = (
        P("seg", "sub", None, None),
        P("seg", "sub", None, None),
        P("seg", "sub", None),
        P(),
        P("seg", "sub"),
        P("seg", "sub", None, None),
        P(),
        P(),
    )
    return jax.shard_map(
        body,
        mesh=mesh,
        in_specs=placed,
        out_specs=(P("seg", "sub", None, None), P("seg", "sub", None, None)),
        check_vma=False,
    )
```
